32 devices in a mesh: outer: 8 (over z, y), inner: 4 (over x, core).
Axes of the slice: x: 2, y: 2, z: 4, core: 2. Of those that a mesh axis runs over, the one named last changes fastest.
Arguments:
- hidden: bfloat16 [4096, 1024], P(('outer', 'inner')), may hold values from -6 to 6
- x_act: bfloat16 [4096, 2048], P(('outer', 'inner')), may hold values from -6 to 6
- dt_step: float32 [4096, 32], P(('outer', 'inner')), may hold values from 0.00421875 to 0.44, as said below
- log_decay: float32 [4096, 32], P(('outer', 'inner')), may hold values from -0.81 to -7.080078e-06, as said below
- w_bc: bfloat16 [1024, 128], P(('outer', 'inner')), may hold values from -0.1875 to 0.1875
- grad_y: bfloat16 [4096, 2048], P(('outer', 'inner')), may hold values from -0.19921875 to 0.19921875
Outputs:
- grad_x: float32 [4096, 2048], P(('outer', 'inner'))
- grad_hidden: float32 [4096, 1024], P(('outer', 'inner'))
- grad_proj: float32 [1024, 128], P(('outer', 'inner'))
The draws below stay inside these ranges and needn't reach their ends.
Inputs may be any that keep to these rules, and one draw needn't show every extreme that they name: `dt_step`: Positive; constant in scale within each head apart from a factor within e**-0.5 to e**0.5. `log_decay`: Negative.
All inputs are finite; a program needn't handle non-finite values.
Results may differ from the reference program's by a relative error of at most 0.0029.
Values may be sent and summed in bfloat16 or wider, within the bound.
No kernel may reach another device: no remote copies, remote signals or barrier semaphores. Data moves between devices by JAX's collectives and lax.ppermute only.
A program may use at most 64 MiB of HBM per device.

```python
import math
import jax
import jax.numpy as jnp
from jax import lax

D = 1024
HEADS = 32
HEAD = 64
STATE = 64
BLOCK = 128
TOK_DEV = 128
TOKENS = 4096


def head_rates(key):
    pick_key = jax.random.fold_in(key, 11)
    slow_key = jax.random.fold_in(key, 12)
    fast_key = jax.random.fold_in(key, 13)
    slow_share = 5
    picks = jax.random.randint(pick_key, (HEADS,), 0, 8)
    slow_rate = jnp.exp(jax.random.uniform(slow_key, (HEADS,), jnp.float32, math.log(0.1), math.log(0.35))) / TOKENS
    fast_rate = jnp.exp(jax.random.uniform(fast_key, (HEADS,), jnp.float32, math.log(0.02), math.log(0.035)))
    return jnp.where(picks < slow_share, slow_rate, fast_rate)


def draw_dt_step(key, part):
    forgetting_speeds = head_rates(key)
    approximate_guess = jax.random.uniform(jax.random.fold_in(key, 21), (TOKENS, HEADS), jnp.float32, -0.5, 0.5)
    return jnp.sqrt(2.0 * forgetting_speeds)[None, :] * jnp.exp(approximate_guess)


def draw_log_decay(key, part):
    forgetting_speeds = head_rates(key)
    blocks = TOKENS // TOK_DEV
    multiplier_coefficient = jnp.exp(jax.random.uniform(jax.random.fold_in(key, 31), (blocks, HEADS), jnp.float32, math.log(0.6), math.log(1.6)))
    multiplier_coefficient = jnp.repeat(multiplier_coefficient, TOK_DEV, axis=0)
    approximate_guess = jnp.exp(jax.random.uniform(jax.random.fold_in(key, 32), (TOKENS, HEADS), jnp.float32, -0.7, 0.7))
    accelerator_slots = jax.random.randint(jax.random.fold_in(key, 33), (2,), 0, TOKENS)
    stack_height = jax.random.uniform(jax.random.fold_in(key, 34), (2, HEADS), jnp.float32, 0.22, 0.69)
    symbol_indices = jnp.arange(TOKENS)[:, None]
    run_span_count = jnp.where(symbol_indices == accelerator_slots[0], stack_height[0][None, :], 0.0) + jnp.where(symbol_indices == accelerator_slots[1], stack_height[1][None, :], 0.0)
    return -(forgetting_speeds[None, :] * multiplier_coefficient * approximate_guess) - run_span_count


def spiked(result, own_key, source, target, shards_of, factor):
    def block_of(position):
        return (jnp.arange(result.shape[position]) // (result.shape[position] // shards_of)).reshape((-1,) + (1,) * (result.ndim - 1 - position))

    near = jax.random.permutation(own_key, shards_of)[block_of(target)]
    far = (block_of(target) + shards_of // 2) % shards_of
    return jnp.where((block_of(source) == near) | (block_of(source) == far), factor * result, result)


def block_levels(own_key, shape, shards, low, high):
    def one(position, parts):
        heights = jax.random.uniform(jax.random.fold_in(jax.random.fold_in(own_key, 6), position), (parts,), jnp.float32, low / len(shards), high / len(shards))
        return jnp.repeat(jnp.exp(heights), shape[position] // parts).reshape((-1,) + (1,) * (len(shape) - position - 1))

    factor_of = one(*shards[0])
    for cut in shards[1:]:
        factor_of = factor_of * one(*cut)
    return factor_of


def scatter_about(key, shape, deviation, bound, cuts=(), dtype=jnp.bfloat16):
    entries = deviation * jax.random.normal(key, shape, jnp.float32)
    if cuts:
        entries = entries * block_levels(key, shape, cuts, -0.22, 0.18)
    return jnp.clip(entries, -bound, bound).astype(dtype)


def heavy_noise(stream_key, dims, scale, bound, split, heavy, kind=jnp.bfloat16):
    array = scale * jax.random.normal(stream_key, dims, jnp.float32)
    if split:
        array = array * block_levels(stream_key, dims, split, -0.22, 0.18)
    return jnp.clip(spiked(array, jax.random.fold_in(stream_key, 3), *heavy), -bound, bound).astype(kind)


def setup_inputs(seed: int = 0) -> dict:
    streams_of = jax.random.split(jax.random.key(seed), 7)
    return {
        "hidden": heavy_noise(streams_of[0], (TOKENS, D), 1.0, 6.0, ((0, 32),), (0, 1, 32, 2.75)),
        "x_act": scatter_about(streams_of[1], (TOKENS, HEADS * HEAD), 1.0, 6.0, ((0, 32),)),
        "dt_step": draw_dt_step(jax.random.fold_in(streams_of[6], 71), 0),
        "log_decay": draw_log_decay(jax.random.fold_in(streams_of[6], 71), 0),
        "w_bc": scatter_about(streams_of[4], (D, 2 * STATE), D ** -0.5, 0.1875, ((0, 32),)),
        "grad_y": scatter_about(streams_of[5], (TOKENS, HEADS * HEAD), 0.03125, 0.19921875, ((0, 32),)),
    }


HIGH = lax.Precision.HIGHEST

def block_step(carried, pieces):
    inputs, decays, b_rows, c_rows = pieces
    length = inputs.shape[0]
    running = jnp.cumsum(decays, axis=0)
    row_ids = lax.broadcasted_iota(jnp.int32, (length, length), 0)
    col_ids = lax.broadcasted_iota(jnp.int32, (length, length), 1)
    causal = row_ids >= col_ids
    spread = running.T[:, :, None] - running.T[:, None, :]
    segment = jnp.where(causal[None], jnp.exp(jnp.where(causal[None], spread, 0.0)), 0.0)
    scores = jnp.einsum('in,jn->ij', c_rows, b_rows, precision=HIGH)
    outputs = jnp.einsum('hij,jhp->ihp', segment * scores[None], inputs, precision=HIGH)
    outputs = outputs + jnp.exp(running)[:, :, None] * jnp.einsum('in,hpn->ihp', c_rows, carried, precision=HIGH)
    final_sum = running[-1]
    weights = jnp.exp(final_sum[None, :] - running)
    updated = jnp.exp(final_sum)[:, None, None] * carried + jnp.einsum('jhp,jn->hpn', inputs * weights[:, :, None], b_rows, precision=HIGH)
    return (updated, outputs)

def scan_block(inputs, decays, b_rows, c_rows, carried, length):
    count = inputs.shape[0] // length
    pieces = (inputs.reshape((count, length) + inputs.shape[1:]), decays.reshape((count, length, decays.shape[1])), b_rows.reshape((count, length, b_rows.shape[1])), c_rows.reshape((count, length, c_rows.shape[1])))
    final_state, outputs = lax.scan(jax.checkpoint(block_step), carried, pieces)
    return (outputs.reshape(inputs.shape), final_state)

def reference(hidden, x_act, dt_step, log_decay, w_bc, grad_y):
    projected = jnp.dot(hidden, w_bc, preferred_element_type=jnp.float32)
    b_rows = projected[:, :STATE]
    c_rows = projected[:, STATE:]
    inputs = dt_step[:, :, None] * x_act.astype(jnp.float32).reshape(TOKENS, HEADS, HEAD)
    cotangent = grad_y.astype(jnp.float32).reshape(TOKENS, HEADS, HEAD)
    start_state = jnp.zeros((HEADS, HEAD, STATE), jnp.float32)

    def forward(inputs, b_rows, c_rows):
        return scan_block(inputs, log_decay, b_rows, c_rows, start_state, BLOCK)[0]
    outputs, pullback = jax.vjp(forward, inputs, b_rows, c_rows)
    d_in, d_b, d_c = pullback(cotangent)
    grad_x = (dt_step[:, :, None] * d_in).reshape(TOKENS, HEADS * HEAD)
    d_proj = jnp.concatenate([d_b, d_c], axis=1)
    d_low = d_proj.astype(jnp.bfloat16)
    grad_hidden = lax.dot_general(d_low, w_bc, (((1,), (1,)), ((), ())), preferred_element_type=jnp.float32)
    grad_proj = lax.dot_general(hidden, d_low, (((0,), (0,)), ((), ())), preferred_element_type=jnp.float32) / math.sqrt(TOKENS)
    return (grad_x, grad_hidden, grad_proj)
```

```python
import functools
import math

import jax
import jax.numpy as jnp
from jax import lax
from jax.experimental import pallas as pl
from jax.experimental.pallas import tpu as pltpu
from jax.sharding import PartitionSpec as P

AXES = ("outer", "inner")
HIGH = lax.Precision.HIGHEST
F32 = jnp.float32
BF16 = jnp.bfloat16
NEG = -1e30
VMEM = pl.BlockSpec(memory_space=pltpu.MemorySpace.VMEM)
SMEM = pl.BlockSpec(memory_space=pltpu.MemorySpace.SMEM)
HBM = pl.BlockSpec(memory_space=pltpu.MemorySpace.HBM)


def call(kernel, name, out_shape, in_specs, scratch=(), out_specs=None):
    return pl.pallas_call(
        kernel,
        name=name,
        out_shape=out_shape,
        in_specs=in_specs,
        out_specs=out_specs or jax.tree.map(lambda _: VMEM, out_shape),
        scratch_shapes=scratch,
        compiler_params=pltpu.CompilerParams(vmem_limit_bytes=16 << 20),
    )


def shaped(shape, dtype):
    return jax.ShapeDtypeStruct(shape, dtype)


def in_hbm(array):
    return pltpu.with_memory_space_constraint(array, pltpu.HBM)


def mm(a, b, precision=None):
    return lax.dot_general(
        a, b, (((1,), (0,)), ((), ())), preferred_element_type=F32, precision=precision
    )


def mm_nt(a, b, precision=None):
    return lax.dot_general(
        a, b, (((1,), (1,)), ((), ())), preferred_element_type=F32, precision=precision
    )


def split(a):
    high = a.astype(BF16)
    return high, (a - high.astype(F32)).astype(BF16)


def iota(shape, dim):
    return lax.broadcasted_iota(jnp.int32, shape, dim)


def spread_kernel(w_hbm, out_hbm, w_ref, out_ref, sems):
    fetch = pltpu.make_async_copy(w_hbm, w_ref, sems.at[0])
    fetch.start()
    fetch.wait()
    out_ref[...] = jnp.broadcast_to(w_ref[...][None], out_ref.shape)
    store = pltpu.make_async_copy(out_ref, out_hbm, sems.at[1])
    store.start()
    store.wait()


def prelude_kernel(x_hbm, grad_hbm, dt_hbm, decay_hbm, hidden_hbm,
                   pair_ref, scaled_hbm, scaled_t_ref, running_t_ref, hidden_t_hbm,
                   x_ref, grad_ref, dt_t_ref, decay_t_ref, hidden_ref, scaled_ref, hidden_t_ref,
                   in_sems, x_sems, grad_sems, out_sems, *, parts):
    heads, rows = dt_t_ref.shape
    size = x_ref.shape[1] // heads
    groups = x_sems.shape[0]
    wide = x_ref.shape[1] // groups
    small = [
        pltpu.make_async_copy(source, target, in_sems.at[k])
        for k, (source, target) in enumerate(
            ((decay_hbm, decay_t_ref), (dt_hbm, dt_t_ref), (hidden_hbm, hidden_ref))
        )
    ]

    def columns(source, target, sems, group):
        lanes = pl.ds(group * wide, wide)
        return pltpu.make_async_copy(source.at[:, lanes], target.at[:, lanes], sems.at[group])

    x_in = [columns(x_hbm, x_ref, x_sems, group) for group in range(groups)]
    grad_in = [columns(grad_hbm, grad_ref, grad_sems, group) for group in range(groups)]
    scaled_out = [columns(scaled_ref, scaled_hbm, out_sems, group) for group in range(groups)]
    hidden_out = pltpu.make_async_copy(hidden_t_ref, hidden_t_hbm, in_sems.at[3])
    for copy in small[:2]:
        copy.start()
    for group in range(groups):
        x_in[group].start()
        grad_in[group].start()
    small[2].start()
    for copy in small[:2]:
        copy.wait()
    causal = iota((rows, rows), 0) >= iota((rows, rows), 1)
    upto = iota((rows, rows), 0) <= iota((rows, rows), 1)
    running_t = mm(decay_t_ref[...], upto.astype(F32), HIGH)
    running_t_ref[...] = running_t
    running = running_t.T
    dt_t = dt_t_ref[...]
    to_end_t = dt_t * jnp.exp(running_t[:, rows - 1 : rows] - running_t)
    to_end = to_end_t.T
    from_start_t = jnp.exp(running_t)
    from_start = jnp.exp(running)
    first = iota((rows, 2 * size), 1) < size
    total = jnp.zeros((rows, rows), F32)
    for pair in range(heads // 2):
        group = 2 * size * pair // wide
        if 2 * size * pair % wide == 0:
            x_in[group].wait()
            grad_in[group].wait()
        lanes = slice(2 * size * pair, 2 * size * (pair + 1))
        even, odd = 2 * pair, 2 * pair + 1
        x = x_ref[:, lanes]
        grad = grad_ref[:, lanes]
        zero = jnp.zeros_like(grad)
        both = jnp.concatenate([jnp.where(first, grad, zero), jnp.where(first, zero, grad)], axis=0)
        products = mm_nt(both, x)
        for place, head in enumerate((even, odd)):
            spread = running[:, head : head + 1] - running_t[head : head + 1, :]
            segment = jnp.exp(jnp.where(causal, spread, NEG))
            part = products[place * rows : (place + 1) * rows, :]
            total = total + segment * (part * dt_t[head : head + 1, :])
        x = x.astype(F32)
        grad = grad.astype(F32)
        x_scale = jnp.where(first, to_end[:, even : even + 1], to_end[:, odd : odd + 1])
        grad_scale = jnp.where(first, from_start[:, even : even + 1], from_start[:, odd : odd + 1])
        x_high, x_low = split(x * x_scale)
        grad_high, grad_low = split(grad * grad_scale)
        for k, value in enumerate((x_high, grad_high, x_low, grad_low)):
            scaled_ref[k * rows : (k + 1) * rows, lanes] = value
        x_t = x.T
        grad_t = grad.T
        for place, head in enumerate((even, odd)):
            here = slice(place * size, (place + 1) * size)
            there = slice(size * head, size * (head + 1))
            x_high, x_low = split(x_t[here, :] * to_end_t[head : head + 1, :])
            grad_high, grad_low = split(grad_t[here, :] * from_start_t[head : head + 1, :])
            for k, value in enumerate((x_high, grad_high, x_low, grad_low)):
                scaled_t_ref[there, k * rows : (k + 1) * rows] = value
        if 2 * size * (pair + 1) % wide == 0:
            scaled_out[group].start()
    pair_ref[...] = total
    small[2].wait()
    if parts:
        count = hidden_ref.shape[1] // parts
        for k in range(0, hidden_ref.shape[1], 128):
            block = hidden_ref[:, k : k + 128].astype(F32).T.astype(BF16)
            for r in range(0, 128, parts):
                piece = (k + r) // parts
                target = ((piece % 2) * (count // 2) + piece // 2) * parts
                hidden_t_ref[target : target + parts, :] = block[r : r + parts, :]
    else:
        hidden_t_ref[...] = jnp.zeros_like(hidden_t_ref)
    hidden_out.start()
    for copy in scaled_out:
        copy.wait()
    hidden_out.wait()


def states_kernel(place_ref, hidden_ref, w_ref, scaled_t_ref, running_t_ref,
                  projected_ref, keep_ref, send_ref, totals_ref):
    rows, width = projected_ref.shape
    heads = running_t_ref.shape[0]
    half = scaled_t_ref.shape[0] // 2
    projected = mm(hidden_ref[...], w_ref[...].reshape(hidden_ref.shape[1], width))
    projected_ref[...] = projected
    first = iota(projected.shape, 1) < width // 2
    blocks = jnp.concatenate(
        [jnp.where(first, projected, 0.0), jnp.where(first, 0.0, projected)], axis=0
    )
    high, low = split(blocks)
    twice = jnp.concatenate([high, high], axis=0)
    totals_ref[...] = jnp.broadcast_to(running_t_ref[:, rows - 1 : rows], (heads, width))
    mine = place_ref[0]
    for which, out_ref in ((1 - mine, send_ref), (mine, keep_ref)):
        scaled = scaled_t_ref[pl.ds(pl.multiple_of(which * half, half), half), :]
        out_ref[0:half, :] = mm(scaled, twice) + mm(scaled[:, 0 : 2 * rows], low)
        out_ref[half:, :] = totals_ref[
            pl.ds(pl.multiple_of(which * (heads // 2), heads // 2), heads // 2), :
        ]


def chip_kernel(place_ref, keep_ref, recv_ref, out_ref, *, size):
    core = place_ref[0]
    chips, chunk, width = out_ref.shape
    rows = chunk - 8
    half = chips * rows
    first_lanes = iota((rows, width), 1) < width // 2
    term = iota((8, width), 0)
    for k in range(chips):
        head = k * rows // size
        here = slice(k * rows, (k + 1) * rows)
        total = slice(half + head, half + head + 1)
        keep = keep_ref[here, :]
        recv = recv_ref[here, :]
        total_kept, total_received = keep_ref[total, :], recv_ref[total, :]
        over_kept, over_received = jnp.exp(total_kept), jnp.exp(total_received)
        as_first = jnp.where(first_lanes, keep * over_received + recv, keep + over_kept * recv)
        as_second = jnp.where(first_lanes, recv * over_kept + keep, recv + over_received * keep)
        out_ref[k, 0:rows, :] = jnp.where(core == 0, as_first, as_second).astype(BF16)
        over = jnp.exp(total_kept + total_received)
        high = over.astype(BF16).astype(F32)
        middle, low = split(over - high)
        terms = jnp.where(term == 0, high, jnp.where(term == 1, middle.astype(F32), low.astype(F32)))
        out_ref[k, rows:, :] = terms.astype(BF16)


def scan_kernel(in_ref, out_ref, before_ref):
    chips, rows, width = out_ref.shape
    first_lanes = iota((rows, width), 1) < width // 2

    def step(k, carried):
        terms = in_ref[k, rows:, :].astype(F32)
        over = terms[0:1, :] + terms[1:2, :] + terms[2:3, :]
        return over * carried + in_ref[k, 0:rows, :].astype(F32)

    def forward(k, carried):
        before_ref[k] = carried
        return step(k, carried)

    def backward(count, carried):
        k = chips - 1 - count
        out_ref[k] = jnp.where(first_lanes, before_ref[k], carried).astype(BF16)
        return step(k, carried)

    start = jnp.zeros((rows, width), F32)
    lax.fori_loop(0, chips, forward, start, unroll=chips <= 16)
    lax.fori_loop(0, chips, backward, start, unroll=chips <= 16)


def core_kernel(place_ref, in_ref, keep_ref, recv_ref, mine_ref, send_ref, *, size):
    core = place_ref[0]
    half, width = in_ref.shape
    plain = iota((size, width), 1) // (width // 2) == core
    for k in range(half // size):
        here = slice(k * size, (k + 1) * size)
        total = slice(half + k, half + k + 1)
        keep = keep_ref[here, :]
        recv = recv_ref[here, :]
        arrived = in_ref[here, :].astype(F32)
        for_mine = recv + jnp.exp(recv_ref[total, :]) * arrived
        for_other = keep + jnp.exp(keep_ref[total, :]) * arrived
        mine_ref[here, :] = jnp.where(plain, arrived, for_mine)
        send_ref[here, :] = jnp.where(plain, for_other, arrived)


def inside_kernel(projected_ref, pair_ref, grad_ref, running_t_ref, d_in_ref, d_proj_ref):
    heads, rows = running_t_ref.shape
    width = projected_ref.shape[1]
    size = grad_ref.shape[1] // heads
    projected = projected_ref[...]
    swapped = pltpu.roll(projected, width // 2, 1)
    first = iota(projected.shape, 1) < width // 2
    scores_t = mm_nt(jnp.where(first, projected, 0.0), swapped, HIGH)
    running_t = running_t_ref[...]
    running = running_t.T
    later = iota((rows, rows), 1) >= iota((rows, rows), 0)
    lanes_first = iota((rows, 2 * size), 1) < size
    for pair in range(heads // 2):
        lanes = slice(2 * size * pair, 2 * size * (pair + 1))
        grad = grad_ref[:, lanes]
        zero = jnp.zeros_like(grad)
        both = jnp.concatenate(
            [jnp.where(lanes_first, grad, zero), jnp.where(lanes_first, zero, grad)], axis=0
        )
        highs, lows = [], []
        for head in (2 * pair, 2 * pair + 1):
            spread = running_t[head : head + 1, :] - running[:, head : head + 1]
            high, low = split(jnp.exp(jnp.where(later, spread, NEG)) * scores_t)
            highs.append(high)
            lows.append(low)
        d_in_ref[:, lanes] = mm(jnp.concatenate(highs, axis=1), both) + mm(
            jnp.concatenate(lows, axis=1), both
        )
    pair_sum = pair_ref[...]
    onto_c = mm(pair_sum, projected, HIGH)
    onto_b = mm(pair_sum.T, projected, HIGH)
    d_proj_ref[...] = pltpu.roll(jnp.where(first, onto_c, onto_b), width // 2, 1)


def project_kernel(place_ref, mine_ref, recv_ref, scaled_ref, d_proj_ref, hidden_t_ref,
                   d_low_ref, keep_ref, send_ref, high_ref, low_ref):
    rows, width = d_proj_ref.shape
    half = mine_ref.shape[0]
    core = place_ref[0]
    for which, in_ref in ((core, mine_ref), (1 - core, recv_ref)):
        there = pl.ds(pl.multiple_of(which * half, half), half)
        high, low = split(in_ref[...])
        high_ref[there, :] = high
        low_ref[there, :] = low
    by_high = mm(scaled_ref[...], high_ref[...])
    by_low = mm(scaled_ref[0 : 2 * rows, :], low_ref[...])
    onto = by_high[0 : 2 * rows, :] + by_high[2 * rows :, :] + by_low
    first = iota((rows, width), 1) < width // 2
    crossing = jnp.where(first, onto[rows:, :], onto[:rows, :])
    d_low = (d_proj_ref[...] + pltpu.roll(crossing, width // 2, 1)).astype(BF16)
    d_low_ref[...] = d_low
    part = send_ref.shape[0]
    for which, out_ref in ((1 - core, send_ref), (core, keep_ref)):
        out_ref[...] = mm(hidden_t_ref[pl.ds(pl.multiple_of(which * part, part), part), :], d_low)


def inputs_kernel(place_ref, mine_ref, recv_ref, projected_ref, d_in_ref, dt_t_ref, running_t_ref,
                  d_low_ref, w_ref, grad_x_ref, grad_hidden_ref, entries_ref):
    half = mine_ref.shape[0]
    core = place_ref[0]
    for which, in_ref in ((core, mine_ref), (1 - core, recv_ref)):
        there = pl.ds(pl.multiple_of(which * half, half), half)
        entries_ref[there, :] = in_ref[...].astype(BF16)
    heads, rows = dt_t_ref.shape
    width = projected_ref.shape[1]
    size = d_in_ref.shape[1] // heads
    grad_hidden_ref[...] = mm_nt(
        d_low_ref[...], w_ref[...].reshape(grad_hidden_ref.shape[1], width)
    )
    swapped = pltpu.roll(projected_ref[...], width // 2, 1)
    first = iota((rows, width), 1) < width // 2
    b_high, b_low = split(jnp.where(first, 0.0, swapped))
    b_both = jnp.concatenate([b_high, b_low], axis=0)
    running_t = running_t_ref[...]
    dt = dt_t_ref[...].T
    to_end = jnp.exp(running_t[:, rows - 1 : rows] - running_t).T
    lanes_first = iota((rows, 2 * size), 1) < size
    for pair in range(heads // 2):
        lanes = slice(2 * size * pair, 2 * size * (pair + 1))
        even, odd = 2 * pair, 2 * pair + 1
        crossing = mm_nt(b_both, entries_ref[lanes, :])
        crossing = crossing[:rows, :] + crossing[rows:, :]
        decay = jnp.where(lanes_first, to_end[:, even : even + 1], to_end[:, odd : odd + 1])
        step = jnp.where(lanes_first, dt[:, even : even + 1], dt[:, odd : odd + 1])
        grad_x_ref[:, lanes] = step * (d_in_ref[:, lanes] + decay * crossing)


def sum_kernel(terms_ref, out_ref, *, scale):
    out_ref[...] = jnp.sum(terms_ref[...], axis=0) * scale


def per_device(hidden, x_act, dt_step, log_decay, w_bc, grad_y):
    devices = lax.axis_size("outer") * lax.axis_size("inner")
    rows, model = hidden.shape
    heads = dt_step.shape[1]
    flat = x_act.shape[1]
    size = flat // heads
    w_rows, width = w_bc.shape
    half = flat // 2
    chips = devices // 2
    slice_rows = half // chips
    position = lax.axis_index("outer") * lax.axis_size("inner") + lax.axis_index("inner")
    place = (position & 1).astype(jnp.int32).reshape(1)
    partner = [(i, i ^ 1) for i in range(devices)]
    same_core = [list(range(core, devices, 2)) for core in range(2)]

    def exchange(array):
        return lax.all_to_all(
            array, AXES, split_axis=0, concat_axis=0, tiled=True, axis_index_groups=same_core
        )

    spread = call(
        spread_kernel, "spread", pltpu.HBM((devices, w_rows, width), BF16), [HBM],
        [pltpu.VMEM((w_rows, width), BF16), pltpu.VMEM((devices, w_rows, width), BF16),
         pltpu.SemaphoreType.DMA((2,))],
        HBM,
    )(in_hbm(w_bc))
    gathered = lax.all_to_all(spread, AXES, split_axis=0, concat_axis=0, tiled=True)
    dt_t = dt_step.T
    in_kernel = w_rows % 16 == 0
    hidden_t_rows = model if in_kernel else 16
    groups = 4
    pair_sum, scaled, scaled_t, running_t, hidden_t = call(
        functools.partial(prelude_kernel, parts=w_rows if in_kernel else 0), "prelude",
        (shaped((rows, rows), F32), pltpu.HBM((4 * rows, flat), BF16), shaped((flat, 4 * rows), BF16),
         shaped((heads, rows), F32), pltpu.HBM((hidden_t_rows, rows), BF16)),
        [HBM] * 5,
        [pltpu.VMEM((rows, flat), BF16), pltpu.VMEM((rows, flat), BF16),
         pltpu.VMEM((heads, rows), F32), pltpu.VMEM((heads, rows), F32),
         pltpu.VMEM((rows, model), BF16), pltpu.VMEM((4 * rows, flat), BF16),
         pltpu.VMEM((hidden_t_rows, rows), BF16)]
        + [pltpu.SemaphoreType.DMA((groups,)) for _ in range(4)],
        (VMEM, HBM, VMEM, VMEM, HBM),
    )(in_hbm(x_act), in_hbm(grad_y), in_hbm(dt_t), in_hbm(log_decay.T), in_hbm(hidden))
    weights = gathered
    if not in_kernel:
        weights = gathered.reshape(model, width)
        hidden_t = hidden.T.reshape(chips, 2, w_rows, rows).transpose(1, 0, 2, 3)
        hidden_t = hidden_t.reshape(model, rows)
    extended = half + heads // 2
    projected, keep, send, _ = call(
        states_kernel, "states",
        (shaped((rows, width), F32), shaped((extended, width), F32), shaped((extended, width), F32),
         shaped((heads, width), F32)),
        [SMEM] + [VMEM] * 4,
    )(place, hidden, weights, scaled_t, running_t)
    recv = lax.ppermute(send, AXES, partner)
    chip_total = call(
        functools.partial(chip_kernel, size=size), "chip",
        shaped((chips, slice_rows + 8, width), BF16), [SMEM, VMEM, VMEM],
    )(place, keep, recv)
    slices = exchange(chip_total)
    d_in, d_proj = call(
        inside_kernel, "inside", (shaped((rows, flat), F32), shaped((rows, width), F32)),
        [VMEM] * 4,
    )(projected, pair_sum, grad_y, running_t)
    around = call(
        scan_kernel, "scan", shaped((chips, slice_rows, width), BF16), [VMEM],
        [pltpu.VMEM((chips, slice_rows, width), F32)],
    )(slices)
    arrived = exchange(around).reshape(half, width)
    mine, send_back = call(
        functools.partial(core_kernel, size=size), "core",
        (shaped((half, width), F32), shaped((half, width), F32)),
        [SMEM, VMEM, VMEM, VMEM],
    )(place, arrived, keep, recv)
    recv_back = lax.ppermute(send_back, AXES, partner)
    d_low, keep_term, send_term = call(
        project_kernel, "project",
        (shaped((rows, width), BF16), shaped((model // 2, width), F32),
         shaped((model // 2, width), F32)),
        [SMEM] + [VMEM] * 5,
        [pltpu.VMEM((flat, width), BF16), pltpu.VMEM((flat, width), BF16)],
    )(place, mine, recv_back, scaled, d_proj, hidden_t)
    recv_term = lax.ppermute(send_term, AXES, partner)
    terms = exchange((keep_term + recv_term).reshape(chips, w_rows, width))
    grad_x, grad_hidden = call(
        inputs_kernel, "inputs", (shaped((rows, flat), F32), shaped((rows, model), F32)),
        [SMEM] + [VMEM] * 8, [pltpu.VMEM((flat, width), BF16)],
    )(place, mine, recv_back, projected, d_in, dt_t, running_t, d_low, weights)
    scale = 1.0 / math.sqrt(rows * devices)
    grad_proj = call(
        functools.partial(sum_kernel, scale=scale), "total", shaped((w_rows, width), F32), [VMEM]
    )(terms)
    return (grad_x, grad_hidden, grad_proj)


def solution(mesh):
    spec = P(AXES, None)
    return jax.shard_map(
        per_device, mesh=mesh, in_specs=(spec,) * 6, out_specs=(spec,) * 3, check_vma=False
    )
```

```python
import functools
import math

import jax
import jax.numpy as jnp
from jax import lax
from jax.experimental import pallas as pl
from jax.experimental.pallas import tpu as pltpu
from jax.sharding import PartitionSpec as P


AXES = ("outer", "inner")
HIGH = lax.Precision.HIGHEST
F32 = jnp.float32
BF16 = jnp.bfloat16
NEG = -1e30
VMEM = pl.BlockSpec(memory_space=pltpu.MemorySpace.VMEM)
SMEM = pl.BlockSpec(memory_space=pltpu.MemorySpace.SMEM)
HBM = pl.BlockSpec(memory_space=pltpu.MemorySpace.HBM)


def call(kernel, out_shape, in_specs, scratch=(), out_specs=None):
    return pl.pallas_call(
        kernel,
        out_shape=out_shape,
        in_specs=in_specs,
        out_specs=out_specs or jax.tree.map(lambda _: VMEM, out_shape),
        scratch_shapes=scratch,
        compiler_params=pltpu.CompilerParams(vmem_limit_bytes=16 << 20),
    )


def shaped(shape, dtype):
    return jax.ShapeDtypeStruct(shape, dtype)


def in_hbm(array):
    return pltpu.with_memory_space_constraint(array, pltpu.HBM)


def mm(a, b, precision=None):
    return lax.dot_general(
        a, b, (((1,), (0,)), ((), ())), preferred_element_type=F32, precision=precision
    )


def mm_nt(a, b, precision=None):
    return lax.dot_general(
        a, b, (((1,), (1,)), ((), ())), preferred_element_type=F32, precision=precision
    )


def split(a):
    high = a.astype(BF16)
    return high, (a - high.astype(F32)).astype(BF16)


def iota(shape, dim):
    return lax.broadcasted_iota(jnp.int32, shape, dim)


def spread_kernel(w_hbm, dt_hbm, decay_hbm, out_hbm, small_ref, w_ref, out_ref, sems):
    fetches = [
        pltpu.make_async_copy(w_hbm, w_ref, sems.at[0]),
        pltpu.make_async_copy(dt_hbm, small_ref.at[0], sems.at[1]),
        pltpu.make_async_copy(decay_hbm, small_ref.at[1], sems.at[2]),
    ]
    for fetch in fetches:
        fetch.start()
    fetches[0].wait()
    out_ref[...] = jnp.broadcast_to(w_ref[...][None], out_ref.shape)
    store = pltpu.make_async_copy(out_ref, out_hbm, sems.at[3])
    store.start()
    for fetch in fetches[1:]:
        fetch.wait()
    store.wait()


def prelude_kernel(place_ref, x_hbm, x_other_hbm, grad_hbm, grad_other_hbm, small_ref,
                   small_other_ref, hidden_hbm, hidden_other_hbm,
                   pair_hbm, scaled_t_ref, running_t_ref, dt_t_hbm, hidden_ref,
                   hidden_t_hbm, x_both_hbm, grad_both_hbm,
                   x_ref, grad_ref, hidden_all_t_ref, hidden_t_ref, pair_ref,
                   dt_t_ref, x_sems, grad_sems, hidden_sems, out_sems, *, parts):
    core = place_ref[0]
    heads, rows = small_ref.shape[1] // 2, small_ref.shape[2]
    tokens = 2 * rows
    half = x_ref.shape[1]
    size = half // heads
    groups = x_sems.shape[1]
    wide = half // groups

    def fetch(sources, target, sems, group):
        copies = []
        for which, source in enumerate(sources):
            there = core if which == 0 else 1 - core
            start = pl.multiple_of(core * half + group * wide, wide)
            copies.append(pltpu.make_async_copy(
                source.at[:, pl.ds(start, wide)],
                target.at[pl.ds(pl.multiple_of(there * rows, rows), rows), pl.ds(group * wide, wide)],
                sems.at[which, group],
            ))
        return copies

    x_in = [fetch((x_hbm, x_other_hbm), x_ref, x_sems, group) for group in range(groups)]
    grad_in = [fetch((grad_hbm, grad_other_hbm), grad_ref, grad_sems, group) for group in range(groups)]
    hidden_in = [
        pltpu.make_async_copy(
            source, hidden_ref.at[pl.ds(pl.multiple_of(there * rows, rows), rows), :],
            hidden_sems.at[k],
        )
        for k, (source, there) in enumerate(((hidden_hbm, core), (hidden_other_hbm, 1 - core)))
    ]
    x_out = pltpu.make_async_copy(x_ref, x_both_hbm, out_sems.at[4])
    grad_out = pltpu.make_async_copy(grad_ref, grad_both_hbm, out_sems.at[0])
    hidden_out = pltpu.make_async_copy(hidden_t_ref, hidden_t_hbm, out_sems.at[1])
    pair_out = pltpu.make_async_copy(pair_ref, pair_hbm, out_sems.at[2])
    dt_out = pltpu.make_async_copy(dt_t_ref, dt_t_hbm, out_sems.at[3])
    for group in range(groups):
        for copy in x_in[group] + grad_in[group]:
            copy.start()
    for copy in hidden_in:
        copy.start()

    mine = pl.ds(pl.multiple_of(core * heads, heads), heads)

    def both_cores(index):
        own, other = small_ref[index, mine, :], small_other_ref[index, mine, :]
        return jnp.concatenate(
            [jnp.where(core == 0, own, other), jnp.where(core == 0, other, own)], axis=1
        )

    dt_t, decay_t = both_cores(0), both_cores(1)
    dt_t_ref[...] = dt_t
    dt_out.start()
    upto = iota((tokens, tokens), 0) <= iota((tokens, tokens), 1)
    running_t = mm(decay_t, upto.astype(F32), HIGH)
    running_t_ref[...] = running_t
    running = running_t.T
    to_end_t = dt_t * jnp.exp(running_t[:, tokens - 1 : tokens] - running_t)
    from_start_t = jnp.exp(running_t)
    causal = iota((rows, rows), 0) >= iota((rows, rows), 1)
    first = iota((tokens, 2 * size), 1) < size
    pair_ref[...] = jnp.zeros_like(pair_ref)
    for pair in range(heads // 2):
        group = 2 * size * pair // wide
        if 2 * size * pair % wide == 0:
            for copy in x_in[group] + grad_in[group]:
                copy.wait()
        lanes = slice(2 * size * pair, 2 * size * (pair + 1))
        even, odd = 2 * pair, 2 * pair + 1
        x = x_ref[:, lanes]
        grad = grad_ref[:, lanes]
        zero = jnp.zeros_like(grad)
        both = jnp.concatenate([jnp.where(first, grad, zero), jnp.where(first, zero, grad)], axis=0)
        products = mm_nt(both, x)
        for at, to in ((0, 0), (1, 0), (1, 1)):
            here, there = slice(at * rows, (at + 1) * rows), slice(to * rows, (to + 1) * rows)
            total = pair_ref[here, there]
            for place, head in enumerate((even, odd)):
                spread = running[here, head : head + 1] - running_t[head : head + 1, there]
                if at == to:
                    spread = jnp.where(causal, spread, NEG)
                start = place * tokens + at * rows
                part = products[start : start + rows, there]
                total = total + jnp.exp(spread) * (part * dt_t[head : head + 1, there])
            pair_ref[here, there] = total
        x_t = x.astype(F32).T
        grad_t = grad.astype(F32).T
        for place, head in enumerate((even, odd)):
            here = slice(place * size, (place + 1) * size)
            there = slice(size * head, size * (head + 1))
            x_high, x_low = split(x_t[here, :] * to_end_t[head : head + 1, :])
            grad_high, grad_low = split(grad_t[here, :] * from_start_t[head : head + 1, :])
            for k, value in enumerate((x_high, grad_high, x_low, grad_low)):
                scaled_t_ref[there, k * tokens : (k + 1) * tokens] = value
    x_out.start()
    grad_out.start()
    pair_out.start()
    for copy in hidden_in:
        copy.wait()
    if parts:
        for k in range(0, hidden_ref.shape[1], 128):
            block = hidden_ref[:, k : k + 128].astype(F32).T
            hidden_all_t_ref[k : k + 128, :] = block.astype(BF16)
        for k in range(hidden_t_ref.shape[0] // parts):
            start = pl.multiple_of((2 * k + core) * parts, parts)
            hidden_t_ref[k * parts : (k + 1) * parts, :] = hidden_all_t_ref[pl.ds(start, parts), :]
    else:
        hidden_t_ref[...] = jnp.zeros_like(hidden_t_ref)
    hidden_out.start()
    for copy in (x_out, grad_out, hidden_out, pair_out, dt_out):
        copy.wait()


def states_kernel(hidden_ref, w_ref, scaled_t_ref, running_t_ref, projected_ref, slices_ref):
    tokens, width = projected_ref.shape
    heads = running_t_ref.shape[0]
    chips, rows = slices_ref.shape[0], slices_ref.shape[1] - 8
    projected = mm(hidden_ref[...], w_ref[...].reshape(hidden_ref.shape[1], width))
    projected_ref[...] = projected
    first = iota(projected.shape, 1) < width // 2
    blocks = jnp.concatenate(
        [jnp.where(first, projected, 0.0), jnp.where(first, 0.0, projected)], axis=0
    )
    high, low = split(blocks)
    states = mm(scaled_t_ref[...], jnp.concatenate([high, high], axis=0))
    states = states + mm(scaled_t_ref[:, 0 : 2 * tokens], low)
    slices_ref[:, 0:rows, :] = states.astype(BF16).reshape(chips, rows, width)
    over = jnp.exp(running_t_ref[:, tokens - 1 : tokens])
    over = jnp.broadcast_to(over, (heads, width))
    high = over.astype(BF16).astype(F32)
    middle, low = split(over - high)
    middle, low = middle.astype(F32), low.astype(F32)
    term = iota((8, width), 0)
    for chip in range(chips):
        head = chip * heads // chips
        line = slice(head, head + 1)
        terms = jnp.where(term == 0, high[line], jnp.where(term == 1, middle[line], low[line]))
        slices_ref[chip, rows:, :] = terms.astype(BF16)


def scan_kernel(in_ref, out_ref, before_ref):
    chips, rows, width = out_ref.shape
    first_lanes = iota((rows, width), 1) < width // 2

    def step(k, carried):
        terms = in_ref[k, rows:, :].astype(F32)
        over = terms[0:1, :] + terms[1:2, :] + terms[2:3, :]
        return over * carried + in_ref[k, 0:rows, :].astype(F32)

    def forward(k, carried):
        before_ref[k] = carried
        return step(k, carried)

    def backward(count, carried):
        k = chips - 1 - count
        out_ref[k] = jnp.where(first_lanes, before_ref[k], carried).astype(BF16)
        return step(k, carried)

    start = jnp.zeros((rows, width), F32)
    lax.fori_loop(0, chips, forward, start, unroll=chips <= 16)
    lax.fori_loop(0, chips, backward, start, unroll=chips <= 16)


def inside_kernel(projected_ref, pair_ref, x_hbm, grad_hbm, dt_t_ref, running_t_ref,
                  d_in_hbm, d_proj_ref, scaled_ref, x_ref, grad_ref, d_in_ref,
                  x_sems, grad_sems, out_sems):
    heads, tokens = running_t_ref.shape
    groups = x_sems.shape[0]
    wide = x_ref.shape[1] // groups

    def columns(source, target, sems, group):
        lanes = pl.ds(group * wide, wide)
        return pltpu.make_async_copy(source.at[:, lanes], target.at[:, lanes], sems.at[group])

    x_in = [columns(x_hbm, x_ref, x_sems, group) for group in range(groups)]
    grad_in = [columns(grad_hbm, grad_ref, grad_sems, group) for group in range(groups)]
    d_in_out = [columns(d_in_ref, d_in_hbm, out_sems, group) for group in range(groups)]
    for group in range(groups):
        grad_in[group].start()
        x_in[group].start()
    rows = tokens // 2
    width = projected_ref.shape[1]
    size = grad_ref.shape[1] // heads
    projected = projected_ref[...]
    swapped = pltpu.roll(projected, width // 2, 1)
    first = iota(projected.shape, 1) < width // 2
    scores_t = mm_nt(jnp.where(first, projected, 0.0), swapped, HIGH)
    running_t = running_t_ref[...]
    running = running_t.T
    to_end = (dt_t_ref[...] * jnp.exp(running_t[:, tokens - 1 : tokens] - running_t)).T
    from_start = jnp.exp(running)
    later = iota((rows, rows), 1) >= iota((rows, rows), 0)
    lanes_first = iota((rows, 2 * size), 1) < size
    all_first = iota((tokens, 2 * size), 1) < size
    for pair in range(heads // 2):
        group = 2 * size * pair // wide
        if 2 * size * pair % wide == 0:
            grad_in[group].wait()
            x_in[group].wait()
        lanes = slice(2 * size * pair, 2 * size * (pair + 1))
        even, odd = 2 * pair, 2 * pair + 1
        x_scale = jnp.where(all_first, to_end[:, even : even + 1], to_end[:, odd : odd + 1])
        grad_scale = jnp.where(
            all_first, from_start[:, even : even + 1], from_start[:, odd : odd + 1]
        )
        x_high, x_low = split(x_ref[:, lanes].astype(F32) * x_scale)
        grad_high, grad_low = split(grad_ref[:, lanes].astype(F32) * grad_scale)
        for k, value in enumerate((x_high, grad_high, x_low, grad_low)):
            scaled_ref[k * tokens : (k + 1) * tokens, lanes] = value
        apart = []
        for part in range(2):
            grad = grad_ref[part * rows : (part + 1) * rows, lanes]
            zero = jnp.zeros_like(grad)
            apart.append((jnp.where(lanes_first, grad, zero), jnp.where(lanes_first, zero, grad)))
        for at in range(2):
            here = slice(at * rows, (at + 1) * rows)
            highs, lows, sources = [], [], []
            for to in range(at, 2):
                there = slice(to * rows, (to + 1) * rows)
                for place, head in enumerate((2 * pair, 2 * pair + 1)):
                    spread = running_t[head : head + 1, there] - running[here, head : head + 1]
                    if at == to:
                        spread = jnp.where(later, spread, NEG)
                    high, low = split(jnp.exp(spread) * scores_t[here, there])
                    highs.append(high)
                    lows.append(low)
                    sources.append(apart[to][place])
            sources = jnp.concatenate(sources, axis=0)
            d_in_ref[here, lanes] = mm(jnp.concatenate(highs, axis=1), sources) + mm(
                jnp.concatenate(lows, axis=1), sources
            )
        if 2 * size * (pair + 1) % wide == 0:
            d_in_out[group].start()
    pair_sum = pair_ref[...]
    onto_c = mm(pair_sum, projected, HIGH)
    onto_b = mm(pair_sum.T, projected, HIGH)
    d_proj_ref[...] = pltpu.roll(jnp.where(first, onto_c, onto_b), width // 2, 1)
    for copy in d_in_out:
        copy.wait()


def cross_kernel(arrived_ref, scaled_ref, d_proj_ref, out_ref):
    tokens, width = d_proj_ref.shape
    onto = mm(scaled_ref[...], arrived_ref[...])
    onto = onto[0 : 2 * tokens, :] + onto[2 * tokens :, :]
    first = iota((tokens, width), 1) < width // 2
    crossing = jnp.where(first, onto[tokens:, :], onto[:tokens, :])
    out_ref[...] = d_proj_ref[...] + pltpu.roll(crossing, width // 2, 1)


def term_kernel(mine_ref, other_ref, hidden_t_ref, d_low_ref, term_hbm, term_ref, sem):
    d_low = (mine_ref[...] + other_ref[...]).astype(BF16)
    d_low_ref[...] = d_low
    term_ref[...] = mm(hidden_t_ref[...], d_low)
    store = pltpu.make_async_copy(term_ref, term_hbm, sem.at[0])
    store.start()
    store.wait()


def inputs_kernel(place_ref, arrived_ref, projected_ref, d_in_hbm, dt_t_ref, running_t_ref,
                  d_low_ref, w_ref, mine_ref, send_ref, grad_hidden_ref, d_in_ref, sems):
    heads, tokens = dt_t_ref.shape
    rows = tokens // 2
    width = projected_ref.shape[1]
    size = d_in_ref.shape[1] // heads
    groups = sems.shape[0]
    wide = d_in_ref.shape[1] // groups
    d_in = []
    for group in range(groups):
        lanes = pl.ds(group * wide, wide)
        d_in.append(pltpu.make_async_copy(d_in_hbm.at[:, lanes], d_in_ref.at[:, lanes], sems.at[group]))
        d_in[group].start()
    own = d_low_ref[pl.ds(pl.multiple_of(place_ref[0] * rows, rows), rows), :]
    grad_hidden_ref[...] = mm_nt(own, w_ref[...].reshape(grad_hidden_ref.shape[1], width))
    core = place_ref[0]
    swapped = pltpu.roll(projected_ref[...], width // 2, 1)
    first = iota((tokens, width), 1) < width // 2
    b_high, b_low = split(jnp.where(first, 0.0, swapped))
    b_both = jnp.concatenate([b_high, b_low], axis=0)
    running_t = running_t_ref[...]
    dt = dt_t_ref[...].T
    to_end = jnp.exp(running_t[:, tokens - 1 : tokens] - running_t).T
    lanes_first = iota((tokens, 2 * size), 1) < size
    for pair in range(heads // 2):
        lanes = slice(2 * size * pair, 2 * size * (pair + 1))
        even, odd = 2 * pair, 2 * pair + 1
        if 2 * size * pair % wide == 0:
            d_in[2 * size * pair // wide].wait()
        crossing = mm_nt(b_both, arrived_ref[lanes, :])
        crossing = crossing[:tokens, :] + crossing[tokens:, :]
        decay = jnp.where(lanes_first, to_end[:, even : even + 1], to_end[:, odd : odd + 1])
        step = jnp.where(lanes_first, dt[:, even : even + 1], dt[:, odd : odd + 1])
        grad = step * (d_in_ref[:, lanes] + decay * crossing)
        mine_ref[:, lanes] = jnp.where(core == 0, grad[:rows, :], grad[rows:, :])
        send_ref[:, lanes] = jnp.where(core == 0, grad[rows:, :], grad[:rows, :])


def join_kernel(place_ref, mine_ref, other_ref, out_hbm, sems):
    core = place_ref[0]
    half = mine_ref.shape[1]
    copies = []
    for k, (source, there) in enumerate(((mine_ref, core), (other_ref, 1 - core))):
        lanes = pl.ds(pl.multiple_of(there * half, half), half)
        copies.append(pltpu.make_async_copy(source, out_hbm.at[:, lanes], sems.at[k]))
    for copy in copies:
        copy.start()
    for copy in copies:
        copy.wait()


def sum_kernel(terms_ref, out_ref, *, scale):
    out_ref[...] = jnp.sum(terms_ref[...], axis=0) * scale


def per_device(hidden, x_act, dt_step, log_decay, w_bc, grad_y):
    devices = lax.axis_size("outer") * lax.axis_size("inner")
    rows, model = hidden.shape
    heads = dt_step.shape[1]
    flat = x_act.shape[1]
    w_rows, width = w_bc.shape
    half = flat // 2
    own_heads = heads // 2
    tokens = 2 * rows
    chips = devices // 2
    slice_rows = half // chips
    position = lax.axis_index("outer") * lax.axis_size("inner") + lax.axis_index("inner")
    place = (position & 1).astype(jnp.int32).reshape(1)
    same_core = [list(range(core, devices, 2)) for core in range(2)]

    def exchange(array):
        return lax.all_to_all(
            array, AXES, split_axis=0, concat_axis=0, tiled=True, axis_index_groups=same_core
        )

    def swap(array):
        return lax.ppermute(array, AXES, [(i, i ^ 1) for i in range(devices)])

    spread, small = call(
        spread_kernel,
        (pltpu.HBM((devices, w_rows, width), BF16), shaped((2, heads, rows), F32)), [HBM] * 3,
        [pltpu.VMEM((w_rows, width), BF16), pltpu.VMEM((devices, w_rows, width), BF16),
         pltpu.SemaphoreType.DMA((4,))],
        (HBM, VMEM),
    )(in_hbm(w_bc), in_hbm(dt_step.T), in_hbm(log_decay.T))
    weights = lax.all_to_all(spread, AXES, split_axis=0, concat_axis=0, tiled=True)
    in_kernel = w_rows % 16 == 0
    groups = 4
    hidden_other = swap(hidden)
    hidden_t_rows = model // 2 if in_kernel else 16
    (pair_sum, scaled_t, running_t, dt_t, hidden_both, hidden_t, x_both, grad_both) = call(
        functools.partial(prelude_kernel, parts=w_rows if in_kernel else 0),
        (pltpu.HBM((tokens, tokens), F32), shaped((half, 4 * tokens), BF16),
         shaped((own_heads, tokens), F32), pltpu.HBM((own_heads, tokens), F32),
         shaped((tokens, model), BF16), pltpu.HBM((hidden_t_rows, tokens), BF16),
         pltpu.HBM((tokens, half), BF16), pltpu.HBM((tokens, half), BF16)),
        [SMEM] + [HBM] * 4 + [VMEM] * 2 + [HBM] * 2,
        [pltpu.VMEM((tokens, half), BF16), pltpu.VMEM((tokens, half), BF16),
         pltpu.VMEM((model, tokens), BF16), pltpu.VMEM((hidden_t_rows, tokens), BF16),
         pltpu.VMEM((tokens, tokens), F32), pltpu.VMEM((own_heads, tokens), F32),
         pltpu.SemaphoreType.DMA((2, groups)), pltpu.SemaphoreType.DMA((2, groups)),
         pltpu.SemaphoreType.DMA((2,)), pltpu.SemaphoreType.DMA((5,))],
        (HBM, VMEM, VMEM, HBM, VMEM, HBM, HBM, HBM),
    )(place, in_hbm(x_act), in_hbm(swap(x_act)), in_hbm(grad_y), in_hbm(swap(grad_y)),
      small, swap(small), in_hbm(hidden), hidden_other)
    if not in_kernel:
        weights = weights.reshape(model, width)
        both = jnp.where(place[0] == 0, jnp.concatenate([hidden, hidden_other], axis=0),
                         jnp.concatenate([hidden_other, hidden], axis=0))
        hidden_t = both.T.reshape(chips, 2, w_rows, tokens)
        hidden_t = jnp.where(place[0] == 0, hidden_t[:, 0], hidden_t[:, 1])
        hidden_t = hidden_t.reshape(model // 2, tokens)
    projected, slices = call(
        states_kernel,
        (shaped((tokens, width), F32), shaped((chips, slice_rows + 8, width), BF16)),
        [VMEM] * 4,
    )(hidden_both, weights, scaled_t, running_t)
    slices = exchange(slices)
    d_in, d_inside, scaled = call(
        inside_kernel,
        (pltpu.HBM((tokens, half), F32), shaped((tokens, width), F32),
         shaped((4 * tokens, half), BF16)),
        [VMEM] * 2 + [HBM] * 2 + [VMEM] * 2,
        [pltpu.VMEM((tokens, half), BF16), pltpu.VMEM((tokens, half), BF16),
         pltpu.VMEM((tokens, half), F32)] + [pltpu.SemaphoreType.DMA((groups,))] * 3,
        (HBM, VMEM, VMEM),
    )(projected, pair_sum, in_hbm(x_both), in_hbm(grad_both), dt_t, running_t)
    around = call(
        scan_kernel, shaped((chips, slice_rows, width), BF16), [VMEM],
        [pltpu.VMEM((chips, slice_rows, width), F32)],
    )(slices)
    arrived = exchange(around).reshape(half, width)
    d_part = call(cross_kernel, shaped((tokens, width), F32), [VMEM] * 3)(arrived, scaled, d_inside)
    d_low, term = call(
        term_kernel,
        (shaped((tokens, width), BF16), pltpu.HBM((model // 2, width), F32)), [VMEM] * 3,
        [pltpu.VMEM((model // 2, width), F32), pltpu.SemaphoreType.DMA((1,))], (VMEM, HBM),
    )(d_part, swap(d_part), hidden_t)
    terms = exchange(term.reshape(chips, w_rows, width))
    mine, send, grad_hidden = call(
        inputs_kernel,
        (shaped((rows, half), F32), shaped((rows, half), F32), shaped((rows, model), F32)),
        [SMEM] + [VMEM] * 2 + [HBM] + [VMEM] * 4,
        [pltpu.VMEM((tokens, half), F32), pltpu.SemaphoreType.DMA((groups,))],
    )(place, arrived, projected, in_hbm(d_in), dt_t, running_t, d_low, weights)
    grad_x = call(
        join_kernel, pltpu.HBM((rows, flat), F32), [SMEM] + [VMEM] * 2,
        [pltpu.SemaphoreType.DMA((2,))], HBM,
    )(place, mine, swap(send))
    scale = 1.0 / math.sqrt(rows * devices)
    grad_proj = call(
        functools.partial(sum_kernel, scale=scale), shaped((w_rows, width), F32), [VMEM]
    )(terms)
    return (grad_x, grad_hidden, grad_proj)


def solution(mesh):
    spec = P(AXES, None)

    return jax.shard_map(
        per_device, mesh=mesh, in_specs=(spec,) * 6, out_specs=(spec,) * 3, check_vma=False
    )
```

```python
import functools
import math

import jax
import jax.numpy as jnp
from jax import lax
from jax.experimental import pallas as pl
from jax.experimental.pallas import tpu as pltpu
from jax.sharding import PartitionSpec as P


AXES = ("outer", "inner")
HIGH = lax.Precision.HIGHEST
F32 = jnp.float32
BF16 = jnp.bfloat16
NEG = -1e30
VMEM = pl.BlockSpec(memory_space=pltpu.MemorySpace.VMEM)
SMEM = pl.BlockSpec(memory_space=pltpu.MemorySpace.SMEM)
HBM = pl.BlockSpec(memory_space=pltpu.MemorySpace.HBM)


def call(kernel, out_shape, in_specs, scratch=(), out_specs=None):
    return pl.pallas_call(
        kernel,
        out_shape=out_shape,
        in_specs=in_specs,
        out_specs=out_specs or jax.tree.map(lambda _: VMEM, out_shape),
        scratch_shapes=scratch,
        compiler_params=pltpu.CompilerParams(vmem_limit_bytes=16 << 20),
    )


def shaped(shape, dtype):
    return jax.ShapeDtypeStruct(shape, dtype)


def in_hbm(array):
    return pltpu.with_memory_space_constraint(array, pltpu.HBM)


def mm(a, b, precision=None):
    return lax.dot_general(
        a, b, (((1,), (0,)), ((), ())), preferred_element_type=F32, precision=precision
    )


def mm_nt(a, b, precision=None):
    return lax.dot_general(
        a, b, (((1,), (1,)), ((), ())), preferred_element_type=F32, precision=precision
    )


def split(a):
    high = a.astype(BF16)
    return high, (a - high.astype(F32)).astype(BF16)


def iota(shape, dim):
    return lax.broadcasted_iota(jnp.int32, shape, dim)


def spread_kernel(w_hbm, dt_hbm, decay_hbm, out_hbm, small_ref, w_ref, out_ref, sems):
    fetches = [
        pltpu.make_async_copy(w_hbm, w_ref, sems.at[0]),
        pltpu.make_async_copy(dt_hbm, small_ref.at[0], sems.at[1]),
        pltpu.make_async_copy(decay_hbm, small_ref.at[1], sems.at[2]),
    ]
    for fetch in fetches:
        fetch.start()
    fetches[0].wait()
    out_ref[...] = jnp.broadcast_to(w_ref[...][None], out_ref.shape)
    store = pltpu.make_async_copy(out_ref, out_hbm, sems.at[3])
    store.start()
    for fetch in fetches[1:]:
        fetch.wait()
    store.wait()


def prelude_kernel(place_ref, x_hbm, x_other_hbm, grad_hbm, grad_other_hbm, small_ref,
                   small_other_ref, hidden_hbm, hidden_other_hbm,
                   pair_hbm, scaled_t_ref, running_t_ref, dt_t_hbm, hidden_ref,
                   hidden_t_hbm, x_both_hbm, grad_both_hbm,
                   x_ref, grad_ref, hidden_all_t_ref, hidden_t_ref, pair_ref,
                   dt_t_ref, x_sems, grad_sems, hidden_sems, out_sems, *, parts):
    core = place_ref[0]
    heads, rows = small_ref.shape[1] // 2, small_ref.shape[2]
    tokens = 2 * rows
    half = x_ref.shape[1]
    size = half // heads
    groups = x_sems.shape[1]
    wide = half // groups

    def fetch(sources, target, sems, group):
        copies = []
        for which, source in enumerate(sources):
            there = core if which == 0 else 1 - core
            start = pl.multiple_of(core * half + group * wide, wide)
            copies.append(pltpu.make_async_copy(
                source.at[:, pl.ds(start, wide)],
                target.at[pl.ds(pl.multiple_of(there * rows, rows), rows), pl.ds(group * wide, wide)],
                sems.at[which, group],
            ))
        return copies

    x_in = [fetch((x_hbm, x_other_hbm), x_ref, x_sems, group) for group in range(groups)]
    grad_in = [fetch((grad_hbm, grad_other_hbm), grad_ref, grad_sems, group) for group in range(groups)]
    hidden_in = [
        pltpu.make_async_copy(
            source, hidden_ref.at[pl.ds(pl.multiple_of(there * rows, rows), rows), :],
            hidden_sems.at[k],
        )
        for k, (source, there) in enumerate(((hidden_hbm, core), (hidden_other_hbm, 1 - core)))
    ]
    x_out = pltpu.make_async_copy(x_ref, x_both_hbm, out_sems.at[4])
    grad_out = pltpu.make_async_copy(grad_ref, grad_both_hbm, out_sems.at[0])
    hidden_out = pltpu.make_async_copy(hidden_t_ref, hidden_t_hbm, out_sems.at[1])
    pair_out = pltpu.make_async_copy(pair_ref, pair_hbm, out_sems.at[2])
    dt_out = pltpu.make_async_copy(dt_t_ref, dt_t_hbm, out_sems.at[3])
    for group in range(groups):
        for copy in x_in[group] + grad_in[group]:
            copy.start()
    for copy in hidden_in:
        copy.start()

    mine = pl.ds(pl.multiple_of(core * heads, heads), heads)

    def both_cores(index):
        own, other = small_ref[index, mine, :], small_other_ref[index, mine, :]
        return jnp.concatenate(
            [jnp.where(core == 0, own, other), jnp.where(core == 0, other, own)], axis=1
        )

    dt_t, decay_t = both_cores(0), both_cores(1)
    dt_t_ref[...] = dt_t
    dt_out.start()
    upto = iota((tokens, tokens), 0) <= iota((tokens, tokens), 1)
    running_t = mm(decay_t, upto.astype(F32), HIGH)
    running_t_ref[...] = running_t
    running = running_t.T
    to_end_t = dt_t * jnp.exp(running_t[:, tokens - 1 : tokens] - running_t)
    from_start_t = jnp.exp(running_t)
    causal = iota((rows, rows), 0) >= iota((rows, rows), 1)
    first = iota((tokens, 2 * size), 1) < size
    pair_ref[...] = jnp.zeros_like(pair_ref)
    for pair in range(heads // 2):
        group = 2 * size * pair // wide
        if 2 * size * pair % wide == 0:
            for copy in x_in[group] + grad_in[group]:
                copy.wait()
        lanes = slice(2 * size * pair, 2 * size * (pair + 1))
        even, odd = 2 * pair, 2 * pair + 1
        x = x_ref[:, lanes]
        grad = grad_ref[:, lanes]
        zero = jnp.zeros_like(grad)
        both = jnp.concatenate([jnp.where(first, grad, zero), jnp.where(first, zero, grad)], axis=0)
        products = mm_nt(both, x)
        for at, to in ((0, 0), (1, 0), (1, 1)):
            here, there = slice(at * rows, (at + 1) * rows), slice(to * rows, (to + 1) * rows)
            total = pair_ref[here, there]
            for place, head in enumerate((even, odd)):
                spread = running[here, head : head + 1] - running_t[head : head + 1, there]
                if at == to:
                    spread = jnp.where(causal, spread, NEG)
                start = place * tokens + at * rows
                part = products[start : start + rows, there]
                total = total + jnp.exp(spread) * (part * dt_t[head : head + 1, there])
            pair_ref[here, there] = total
        x_t = x.astype(F32).T
        grad_t = grad.astype(F32).T
        for place, head in enumerate((even, odd)):
            here = slice(place * size, (place + 1) * size)
            there = slice(size * head, size * (head + 1))
            x_high, x_low = split(x_t[here, :] * to_end_t[head : head + 1, :])
            grad_high, grad_low = split(grad_t[here, :] * from_start_t[head : head + 1, :])
            for k, value in enumerate((x_high, grad_high, x_low, grad_low)):
                scaled_t_ref[there, k * tokens : (k + 1) * tokens] = value
    x_out.start()
    grad_out.start()
    pair_out.start()
    for copy in hidden_in:
        copy.wait()
    if parts:
        for k in range(0, hidden_ref.shape[1], 128):
            block = hidden_ref[:, k : k + 128].astype(F32).T
            hidden_all_t_ref[k : k + 128, :] = block.astype(BF16)
        for k in range(hidden_t_ref.shape[0] // parts):
            start = pl.multiple_of((2 * k + core) * parts, parts)
            hidden_t_ref[k * parts : (k + 1) * parts, :] = hidden_all_t_ref[pl.ds(start, parts), :]
    else:
        hidden_t_ref[...] = jnp.zeros_like(hidden_t_ref)
    hidden_out.start()
    for copy in (x_out, grad_out, hidden_out, pair_out, dt_out):
        copy.wait()


def states_kernel(hidden_ref, w_ref, scaled_t_ref, running_t_ref, projected_ref, slices_ref):
    tokens, width = projected_ref.shape
    heads = running_t_ref.shape[0]
    chips, rows = slices_ref.shape[0], slices_ref.shape[1] - 8
    projected = mm(hidden_ref[...], w_ref[...].reshape(hidden_ref.shape[1], width))
    projected_ref[...] = projected
    first = iota(projected.shape, 1) < width // 2
    blocks = jnp.concatenate(
        [jnp.where(first, projected, 0.0), jnp.where(first, 0.0, projected)], axis=0
    )
    high, low = split(blocks)
    states = mm(scaled_t_ref[...], jnp.concatenate([high, high], axis=0))
    states = states + mm(scaled_t_ref[:, 0 : 2 * tokens], low)
    slices_ref[:, 0:rows, :] = states.astype(BF16).reshape(chips, rows, width)
    over = jnp.exp(running_t_ref[:, tokens - 1 : tokens])
    over = jnp.broadcast_to(over, (heads, width))
    high = over.astype(BF16).astype(F32)
    middle, low = split(over - high)
    middle, low = middle.astype(F32), low.astype(F32)
    term = iota((8, width), 0)
    for chip in range(chips):
        head = chip * heads // chips
        line = slice(head, head + 1)
        terms = jnp.where(term == 0, high[line], jnp.where(term == 1, middle[line], low[line]))
        slices_ref[chip, rows:, :] = terms.astype(BF16)


def scan_kernel(in_ref, out_hbm, before_ref, out_ref, sems):
    chips, rows, width = out_ref.shape
    first_lanes = iota((rows, width), 1) < width // 2

    def step(k, carried):
        terms = in_ref[k, rows:, :].astype(F32)
        over = terms[0:1, :] + terms[1:2, :] + terms[2:3, :]
        return over * carried + in_ref[k, 0:rows, :].astype(F32)

    def forward(k, carried):
        before_ref[k] = carried
        return step(k, carried)

    def backward(count, carried):
        k = chips - 1 - count
        out_ref[k] = jnp.where(first_lanes, before_ref[k], carried).astype(BF16)
        store(k).start()
        return step(k, carried)

    def store(k):
        return pltpu.make_async_copy(out_ref.at[k], out_hbm.at[k], sems.at[k])

    def finish(k, _):
        store(k).wait()
        return 0

    start = jnp.zeros((rows, width), F32)
    lax.fori_loop(0, chips, forward, start, unroll=chips <= 16)
    lax.fori_loop(0, chips, backward, start, unroll=chips <= 16)
    lax.fori_loop(0, chips, finish, 0, unroll=chips <= 16)


def inside_kernel(projected_ref, pair_ref, x_hbm, grad_hbm, dt_t_ref, running_t_ref,
                  d_in_hbm, d_proj_ref, scaled_ref, x_ref, grad_ref, d_in_ref,
                  x_sems, grad_sems, out_sems):
    heads, tokens = running_t_ref.shape
    groups = x_sems.shape[0]
    wide = x_ref.shape[1] // groups

    def columns(source, target, sems, group):
        lanes = pl.ds(group * wide, wide)
        return pltpu.make_async_copy(source.at[:, lanes], target.at[:, lanes], sems.at[group])

    x_in = [columns(x_hbm, x_ref, x_sems, group) for group in range(groups)]
    grad_in = [columns(grad_hbm, grad_ref, grad_sems, group) for group in range(groups)]
    d_in_out = [columns(d_in_ref, d_in_hbm, out_sems, group) for group in range(groups)]
    for group in range(groups):
        grad_in[group].start()
        x_in[group].start()
    rows = tokens // 2
    width = projected_ref.shape[1]
    size = grad_ref.shape[1] // heads
    projected = projected_ref[...]
    swapped = pltpu.roll(projected, width // 2, 1)
    first = iota(projected.shape, 1) < width // 2
    scores_t = mm_nt(jnp.where(first, projected, 0.0), swapped, HIGH)
    running_t = running_t_ref[...]
    running = running_t.T
    to_end = (dt_t_ref[...] * jnp.exp(running_t[:, tokens - 1 : tokens] - running_t)).T
    from_start = jnp.exp(running)
    later = iota((rows, rows), 1) >= iota((rows, rows), 0)
    lanes_first = iota((rows, 2 * size), 1) < size
    all_first = iota((tokens, 2 * size), 1) < size
    for pair in range(heads // 2):
        group = 2 * size * pair // wide
        if 2 * size * pair % wide == 0:
            grad_in[group].wait()
            x_in[group].wait()
        lanes = slice(2 * size * pair, 2 * size * (pair + 1))
        even, odd = 2 * pair, 2 * pair + 1
        x_scale = jnp.where(all_first, to_end[:, even : even + 1], to_end[:, odd : odd + 1])
        grad_scale = jnp.where(
            all_first, from_start[:, even : even + 1], from_start[:, odd : odd + 1]
        )
        x_high, x_low = split(x_ref[:, lanes].astype(F32) * x_scale)
        grad_high, grad_low = split(grad_ref[:, lanes].astype(F32) * grad_scale)
        for k, value in enumerate((x_high, grad_high, x_low, grad_low)):
            scaled_ref[k * tokens : (k + 1) * tokens, lanes] = value
        apart = []
        for part in range(2):
            grad = grad_ref[part * rows : (part + 1) * rows, lanes]
            zero = jnp.zeros_like(grad)
            apart.append((jnp.where(lanes_first, grad, zero), jnp.where(lanes_first, zero, grad)))
        for at in range(2):
            here = slice(at * rows, (at + 1) * rows)
            highs, lows, sources = [], [], []
            for to in range(at, 2):
                there = slice(to * rows, (to + 1) * rows)
                for place, head in enumerate((2 * pair, 2 * pair + 1)):
                    spread = running_t[head : head + 1, there] - running[here, head : head + 1]
                    if at == to:
                        spread = jnp.where(later, spread, NEG)
                    high, low = split(jnp.exp(spread) * scores_t[here, there])
                    highs.append(high)
                    lows.append(low)
                    sources.append(apart[to][place])
            sources = jnp.concatenate(sources, axis=0)
            d_in_ref[here, lanes] = mm(jnp.concatenate(highs, axis=1), sources) + mm(
                jnp.concatenate(lows, axis=1), sources
            )
        if 2 * size * (pair + 1) % wide == 0:
            d_in_out[group].start()
    pair_sum = pair_ref[...]
    onto_c = mm(pair_sum, projected, HIGH)
    onto_b = mm(pair_sum.T, projected, HIGH)
    d_proj_ref[...] = pltpu.roll(jnp.where(first, onto_c, onto_b), width // 2, 1)
    for copy in d_in_out:
        copy.wait()


def cross_kernel(arrived_ref, scaled_ref, d_proj_ref, out_ref):
    tokens, width = d_proj_ref.shape
    onto = mm(scaled_ref[...], arrived_ref[...])
    onto = onto[0 : 2 * tokens, :] + onto[2 * tokens :, :]
    first = iota((tokens, width), 1) < width // 2
    crossing = jnp.where(first, onto[tokens:, :], onto[:tokens, :])
    out_ref[...] = d_proj_ref[...] + pltpu.roll(crossing, width // 2, 1)


def term_kernel(mine_ref, other_ref, hidden_t_ref, d_low_ref, term_hbm, term_ref, sems):
    chips, chunk, _ = term_ref.shape
    rows = hidden_t_ref.shape[0] // chips
    d_low = (mine_ref[...] + other_ref[...]).astype(BF16)
    d_low_ref[...] = d_low
    parts = sems.shape[0]
    stores = []
    for part in range(parts):
        first, count = part * chips // parts, chips // parts
        term = mm(hidden_t_ref[first * rows : (first + count) * rows, :], d_low)
        for k in range(count):
            block = term[k * rows : (k + 1) * rows, :]
            high = block.astype(BF16).astype(F32)
            rest = (block - high)[0 : chunk - rows, :]
            term_ref[first + k] = jnp.concatenate([high, rest], axis=0).astype(BF16)
        there = pl.ds(first, count)
        stores.append(pltpu.make_async_copy(term_ref.at[there], term_hbm.at[there], sems.at[part]))
        stores[-1].start()
    for store in stores:
        store.wait()


def inputs_kernel(place_ref, arrived_ref, projected_ref, d_in_hbm, dt_t_ref, running_t_ref, *rest, other):
    if other:
        grad_ref, d_in_ref, sems = rest
    else:
        d_low_ref, w_ref, grad_ref, grad_hidden_ref, d_in_ref, sems = rest
    heads, tokens = dt_t_ref.shape
    rows = tokens // 2
    width = projected_ref.shape[1]
    size = d_in_ref.shape[1] // heads
    which = 1 - place_ref[0] if other else place_ref[0]
    here = pl.ds(pl.multiple_of(which * rows, rows), rows)
    groups = sems.shape[0]
    wide = d_in_ref.shape[1] // groups
    d_in = []
    for group in range(groups):
        lanes = pl.ds(group * wide, wide)
        d_in.append(pltpu.make_async_copy(d_in_hbm.at[here, lanes], d_in_ref.at[:, lanes], sems.at[group]))
        d_in[group].start()
    if not other:
        grad_hidden_ref[...] = mm_nt(
            d_low_ref[here, :], w_ref[...].reshape(grad_hidden_ref.shape[1], width)
        )
    swapped = pltpu.roll(projected_ref[here, :], width // 2, 1)
    first = iota((rows, width), 1) < width // 2
    b_high, b_low = split(jnp.where(first, 0.0, swapped))
    b_both = jnp.concatenate([b_high, b_low], axis=0)
    running_t = running_t_ref[...]
    to_end_t = jnp.exp(running_t[:, tokens - 1 : tokens] - running_t)

    def columns(both):
        return jnp.where(which == 0, both[:, :rows], both[:, rows:]).T

    dt, to_end = columns(dt_t_ref[...]), columns(to_end_t)
    lanes_first = iota((rows, 2 * size), 1) < size
    for pair in range(heads // 2):
        lanes = slice(2 * size * pair, 2 * size * (pair + 1))
        even, odd = 2 * pair, 2 * pair + 1
        if 2 * size * pair % wide == 0:
            d_in[2 * size * pair // wide].wait()
        crossing = mm_nt(b_both, arrived_ref[lanes, :])
        crossing = crossing[:rows, :] + crossing[rows:, :]
        decay = jnp.where(lanes_first, to_end[:, even : even + 1], to_end[:, odd : odd + 1])
        step = jnp.where(lanes_first, dt[:, even : even + 1], dt[:, odd : odd + 1])
        grad_ref[:, lanes] = step * (d_in_ref[:, lanes] + decay * crossing)


def join_kernel(place_ref, mine_ref, other_ref, out_hbm, sems):
    core = place_ref[0]
    half = mine_ref.shape[1]
    copies = []
    for k, (source, there) in enumerate(((mine_ref, core), (other_ref, 1 - core))):
        lanes = pl.ds(pl.multiple_of(there * half, half), half)
        copies.append(pltpu.make_async_copy(source, out_hbm.at[:, lanes], sems.at[k]))
    for copy in copies:
        copy.start()
    for copy in copies:
        copy.wait()


def sum_kernel(terms_ref, out_ref, *, scale):
    rows = out_ref.shape[0]
    more = terms_ref.shape[1] - rows
    terms = jnp.sum(terms_ref[...].astype(F32), axis=0)
    out_ref[0:more, :] = (terms[0:more, :] + terms[rows:, :]) * scale
    out_ref[more:, :] = terms[more:rows, :] * scale


def per_device(hidden, x_act, dt_step, log_decay, w_bc, grad_y):
    devices = lax.axis_size("outer") * lax.axis_size("inner")
    rows, model = hidden.shape
    heads = dt_step.shape[1]
    flat = x_act.shape[1]
    w_rows, width = w_bc.shape
    half = flat // 2
    own_heads = heads // 2
    tokens = 2 * rows
    chips = devices // 2
    slice_rows = half // chips
    position = lax.axis_index("outer") * lax.axis_size("inner") + lax.axis_index("inner")
    place = (position & 1).astype(jnp.int32).reshape(1)
    same_core = [list(range(core, devices, 2)) for core in range(2)]

    def exchange(array):
        return lax.all_to_all(
            array, AXES, split_axis=0, concat_axis=0, tiled=True, axis_index_groups=same_core
        )

    def swap(array):
        return lax.ppermute(array, AXES, [(i, i ^ 1) for i in range(devices)])

    spread, small = call(
        spread_kernel,
        (pltpu.HBM((devices, w_rows, width), BF16), shaped((2, heads, rows), F32)), [HBM] * 3,
        [pltpu.VMEM((w_rows, width), BF16), pltpu.VMEM((devices, w_rows, width), BF16),
         pltpu.SemaphoreType.DMA((4,))],
        (HBM, VMEM),
    )(in_hbm(w_bc), in_hbm(dt_step.T), in_hbm(log_decay.T))
    weights = lax.all_to_all(spread, AXES, split_axis=0, concat_axis=0, tiled=True)
    in_kernel = w_rows % 16 == 0
    groups = 4
    hidden_other = swap(hidden)
    hidden_t_rows = model // 2 if in_kernel else 16
    (pair_sum, scaled_t, running_t, dt_t, hidden_both, hidden_t, x_both, grad_both) = call(
        functools.partial(prelude_kernel, parts=w_rows if in_kernel else 0),
        (pltpu.HBM((tokens, tokens), F32), shaped((half, 4 * tokens), BF16),
         shaped((own_heads, tokens), F32), pltpu.HBM((own_heads, tokens), F32),
         shaped((tokens, model), BF16), pltpu.HBM((hidden_t_rows, tokens), BF16),
         pltpu.HBM((tokens, half), BF16), pltpu.HBM((tokens, half), BF16)),
        [SMEM] + [HBM] * 4 + [VMEM] * 2 + [HBM] * 2,
        [pltpu.VMEM((tokens, half), BF16), pltpu.VMEM((tokens, half), BF16),
         pltpu.VMEM((model, tokens), BF16), pltpu.VMEM((hidden_t_rows, tokens), BF16),
         pltpu.VMEM((tokens, tokens), F32), pltpu.VMEM((own_heads, tokens), F32),
         pltpu.SemaphoreType.DMA((2, groups)), pltpu.SemaphoreType.DMA((2, groups)),
         pltpu.SemaphoreType.DMA((2,)), pltpu.SemaphoreType.DMA((5,))],
        (HBM, VMEM, VMEM, HBM, VMEM, HBM, HBM, HBM),
    )(place, in_hbm(x_act), in_hbm(swap(x_act)), in_hbm(grad_y), in_hbm(swap(grad_y)),
      small, swap(small), in_hbm(hidden), hidden_other)
    if not in_kernel:
        weights = weights.reshape(model, width)
        both = jnp.where(place[0] == 0, jnp.concatenate([hidden, hidden_other], axis=0),
                         jnp.concatenate([hidden_other, hidden], axis=0))
        hidden_t = both.T.reshape(chips, 2, w_rows, tokens)
        hidden_t = jnp.where(place[0] == 0, hidden_t[:, 0], hidden_t[:, 1])
        hidden_t = hidden_t.reshape(model // 2, tokens)
    projected, slices = call(
        states_kernel,
        (shaped((tokens, width), F32), shaped((chips, slice_rows + 8, width), BF16)),
        [VMEM] * 4,
    )(hidden_both, weights, scaled_t, running_t)
    slices = exchange(slices)
    d_in, d_inside, scaled = call(
        inside_kernel,
        (pltpu.HBM((tokens, half), F32), shaped((tokens, width), F32),
         shaped((4 * tokens, half), BF16)),
        [VMEM] * 2 + [HBM] * 2 + [VMEM] * 2,
        [pltpu.VMEM((tokens, half), BF16), pltpu.VMEM((tokens, half), BF16),
         pltpu.VMEM((tokens, half), F32)] + [pltpu.SemaphoreType.DMA((groups,))] * 3,
        (HBM, VMEM, VMEM),
    )(projected, pair_sum, in_hbm(x_both), in_hbm(grad_both), dt_t, running_t)
    around = call(
        scan_kernel, pltpu.HBM((chips, slice_rows, width), BF16), [VMEM],
        [pltpu.VMEM((chips, slice_rows, width), F32), pltpu.VMEM((chips, slice_rows, width), BF16),
         pltpu.SemaphoreType.DMA((chips,))],
        HBM,
    )(slices)
    arrived = exchange(around).reshape(half, width)
    d_part = call(cross_kernel, shaped((tokens, width), F32), [VMEM] * 3)(arrived, scaled, d_inside)
    term_rows = w_rows + w_rows // 2
    d_low, term = call(
        term_kernel,
        (shaped((tokens, width), BF16), pltpu.HBM((chips, term_rows, width), BF16)), [VMEM] * 3,
        [pltpu.VMEM((chips, term_rows, width), BF16), pltpu.SemaphoreType.DMA((4,))], (VMEM, HBM),
    )(d_part, swap(d_part), hidden_t)
    terms = exchange(term)
    d_in = in_hbm(d_in)
    in_specs = [SMEM] + [VMEM] * 2 + [HBM] + [VMEM] * 2
    scratch = [pltpu.VMEM((rows, half), F32), pltpu.SemaphoreType.DMA((groups,))]
    send = call(
        functools.partial(inputs_kernel, other=True), shaped((rows, half), F32), in_specs,
        scratch,
    )(place, arrived, projected, d_in, dt_t, running_t)
    come = swap(send)
    mine, grad_hidden = call(
        functools.partial(inputs_kernel, other=False),
        (shaped((rows, half), F32), shaped((rows, model), F32)), in_specs + [VMEM] * 2, scratch,
    )(place, arrived, projected, d_in, dt_t, running_t, d_low, weights)
    grad_x = call(
        join_kernel, pltpu.HBM((rows, flat), F32), [SMEM] + [VMEM] * 2,
        [pltpu.SemaphoreType.DMA((2,))], HBM,
    )(place, mine, come)
    scale = 1.0 / math.sqrt(rows * devices)
    grad_proj = call(
        functools.partial(sum_kernel, scale=scale), shaped((w_rows, width), F32), [VMEM]
    )(terms)
    return (grad_x, grad_hidden, grad_proj)


def solution(mesh):
    spec = P(AXES, None)

    return jax.shard_map(
        per_device, mesh=mesh, in_specs=(spec,) * 6, out_specs=(spec,) * 3, check_vma=False
    )
```

```python
import functools
import math

import jax
import jax.numpy as jnp
from jax import lax
from jax.experimental import pallas as pl
from jax.experimental.pallas import tpu as pltpu
from jax.sharding import PartitionSpec as P


AXES = ("outer", "inner")
HIGH = lax.Precision.HIGHEST
F32 = jnp.float32
BF16 = jnp.bfloat16
NEG = -1e30
VMEM = pl.BlockSpec(memory_space=pltpu.MemorySpace.VMEM)
SMEM = pl.BlockSpec(memory_space=pltpu.MemorySpace.SMEM)
HBM = pl.BlockSpec(memory_space=pltpu.MemorySpace.HBM)


def call(kernel, out_shape, in_specs, scratch=(), out_specs=None):
    return pl.pallas_call(
        kernel,
        out_shape=out_shape,
        in_specs=in_specs,
        out_specs=out_specs or jax.tree.map(lambda _: VMEM, out_shape),
        scratch_shapes=scratch,
        compiler_params=pltpu.CompilerParams(vmem_limit_bytes=16 << 20),
    )


def shaped(shape, dtype):
    return jax.ShapeDtypeStruct(shape, dtype)


def in_hbm(array):
    return pltpu.with_memory_space_constraint(array, pltpu.HBM)


def mm(a, b, precision=None):
    return lax.dot_general(
        a, b, (((1,), (0,)), ((), ())), preferred_element_type=F32, precision=precision
    )


def mm_nt(a, b, precision=None):
    return lax.dot_general(
        a, b, (((1,), (1,)), ((), ())), preferred_element_type=F32, precision=precision
    )


def split(a):
    high = a.astype(BF16)
    return high, (a - high.astype(F32)).astype(BF16)


def terms_of(decays, rows):
    count, width = decays.shape
    high = decays.astype(BF16).astype(F32)
    middle, low = split(decays - high)
    rest = jnp.zeros((rows - 3 * count, width), F32)
    return jnp.concatenate([high, middle.astype(F32), low.astype(F32), rest], axis=0)


def from_terms(terms, count):
    terms = terms.astype(F32)
    return terms[0:count, :] + terms[count : 2 * count, :] + terms[2 * count : 3 * count, :]


def iota(shape, dim):
    return lax.broadcasted_iota(jnp.int32, shape, dim)


def spread_kernel(w_hbm, dt_hbm, decay_hbm, out_hbm, small_ref, w_ref, out_ref, sems):
    fetches = [
        pltpu.make_async_copy(w_hbm, w_ref, sems.at[0]),
        pltpu.make_async_copy(dt_hbm, small_ref.at[0], sems.at[1]),
        pltpu.make_async_copy(decay_hbm, small_ref.at[1], sems.at[2]),
    ]
    for fetch in fetches:
        fetch.start()
    fetches[0].wait()
    out_ref[...] = jnp.broadcast_to(w_ref[...][None], out_ref.shape)
    store = pltpu.make_async_copy(out_ref, out_hbm, sems.at[3])
    store.start()
    for fetch in fetches[1:]:
        fetch.wait()
    store.wait()


def prelude_kernel(place_ref, x_hbm, x_other_hbm, grad_hbm, grad_other_hbm, small_ref,
                   small_other_ref, hidden_hbm, hidden_other_hbm,
                   scaled_t_ref, running_t_ref, dt_t_hbm, hidden_ref,
                   hidden_t_hbm, x_both_hbm, grad_both_hbm,
                   x_ref, grad_ref, hidden_all_t_ref, hidden_t_ref, dt_t_ref,
                    x_sems, grad_sems, hidden_sems, out_sems, *, parts):
    core = place_ref[0] & 1
    heads, rows = small_ref.shape[1] // 2, small_ref.shape[2]
    tokens = 2 * rows
    half = x_ref.shape[1]
    size = half // heads
    groups = x_sems.shape[1]
    wide = half // groups

    def fetch(sources, target, sems, group):
        copies = []
        for which, source in enumerate(sources):
            there = core if which == 0 else 1 - core
            start = pl.multiple_of(core * half + group * wide, wide)
            copies.append(pltpu.make_async_copy(
                source.at[:, pl.ds(start, wide)],
                target.at[pl.ds(pl.multiple_of(there * rows, rows), rows), pl.ds(group * wide, wide)],
                sems.at[which, group],
            ))
        return copies

    x_in = [fetch((x_hbm, x_other_hbm), x_ref, x_sems, group) for group in range(groups)]
    grad_in = [fetch((grad_hbm, grad_other_hbm), grad_ref, grad_sems, group) for group in range(groups)]
    hidden_in = [
        pltpu.make_async_copy(
            source, hidden_ref.at[pl.ds(pl.multiple_of(there * rows, rows), rows), :],
            hidden_sems.at[k],
        )
        for k, (source, there) in enumerate(((hidden_hbm, core), (hidden_other_hbm, 1 - core)))
    ]
    x_out = pltpu.make_async_copy(x_ref, x_both_hbm, out_sems.at[2])
    grad_out = pltpu.make_async_copy(grad_ref, grad_both_hbm, out_sems.at[0])
    hidden_out = pltpu.make_async_copy(hidden_t_ref, hidden_t_hbm, out_sems.at[1])
    dt_out = pltpu.make_async_copy(dt_t_ref, dt_t_hbm, out_sems.at[3])
    for group in range(groups):
        for copy in x_in[group] + grad_in[group]:
            copy.start()
    for copy in hidden_in:
        copy.start()

    mine = pl.ds(pl.multiple_of(core * heads, heads), heads)

    def both_cores(index):
        own, other = small_ref[index, mine, :], small_other_ref[index, mine, :]
        return jnp.concatenate(
            [jnp.where(core == 0, own, other), jnp.where(core == 0, other, own)], axis=1
        )

    dt_t, decay_t = both_cores(0), both_cores(1)
    dt_t_ref[...] = dt_t
    dt_out.start()
    upto = iota((tokens, tokens), 0) <= iota((tokens, tokens), 1)
    running_t = mm(decay_t, upto.astype(F32), HIGH)
    running_t_ref[...] = running_t
    to_end_t = dt_t * jnp.exp(running_t[:, tokens - 1 : tokens] - running_t)
    from_start_t = jnp.exp(running_t)
    for pair in range(heads // 2):
        group = 2 * size * pair // wide
        if 2 * size * pair % wide == 0:
            for copy in x_in[group] + grad_in[group]:
                copy.wait()
        lanes = slice(2 * size * pair, 2 * size * (pair + 1))
        even, odd = 2 * pair, 2 * pair + 1
        x = x_ref[:, lanes]
        grad = grad_ref[:, lanes]
        x_t = x.astype(F32).T
        grad_t = grad.astype(F32).T
        for place, head in enumerate((even, odd)):
            here = slice(place * size, (place + 1) * size)
            there = slice(size * head, size * (head + 1))
            x_high, x_low = split(x_t[here, :] * to_end_t[head : head + 1, :])
            grad_high, grad_low = split(grad_t[here, :] * from_start_t[head : head + 1, :])
            for k, value in enumerate((x_high, grad_high, x_low, grad_low)):
                scaled_t_ref[there, k * tokens : (k + 1) * tokens] = value
    x_out.start()
    grad_out.start()
    for copy in hidden_in:
        copy.wait()
    if parts:
        for k in range(0, hidden_ref.shape[1], 128):
            block = hidden_ref[:, k : k + 128].astype(F32).T
            hidden_all_t_ref[k : k + 128, :] = block.astype(BF16)
        for k in range(hidden_t_ref.shape[0] // parts):
            start = pl.multiple_of((2 * k + core) * parts, parts)
            hidden_t_ref[k * parts : (k + 1) * parts, :] = hidden_all_t_ref[pl.ds(start, parts), :]
    else:
        hidden_t_ref[...] = jnp.zeros_like(hidden_t_ref)
    hidden_out.start()
    for copy in (x_out, grad_out, hidden_out, dt_out):
        copy.wait()


def states_kernel(hidden_ref, w_ref, scaled_t_ref, running_t_ref, projected_ref, slices_ref):
    tokens, width = projected_ref.shape
    heads = running_t_ref.shape[0]
    pieces, piece = slices_ref.shape[0], scaled_t_ref.shape[0] // slices_ref.shape[0]
    projected = mm(hidden_ref[...], w_ref[...].reshape(hidden_ref.shape[1], width))
    projected_ref[...] = projected
    first = iota(projected.shape, 1) < width // 2
    blocks = jnp.concatenate(
        [jnp.where(first, projected, 0.0), jnp.where(first, 0.0, projected)], axis=0
    )
    high, low = split(blocks)
    states = mm(scaled_t_ref[:, 0 : 2 * tokens], jnp.concatenate([high, low], axis=1))
    states = states[:, :width] + states[:, width:] + mm(scaled_t_ref[:, 2 * tokens :], high)
    slices_ref[:, 0:piece, :] = states.reshape(pieces, piece, width)
    over = jnp.exp(running_t_ref[:, tokens - 1 : tokens])
    over = jnp.broadcast_to(over, (heads, width))
    count = heads // pieces
    for k in range(pieces):
        slices_ref[k, piece:, :] = terms_of(
            over[k * count : (k + 1) * count, :], slices_ref.shape[1] - piece
        )


def group_kernel(in_ref, total_ref, inner_ref, decays_ref, send_ref, *, size):
    piece, width = total_ref.shape
    members = in_ref.shape[0]
    count = piece // size
    over = [from_terms(in_ref[member, piece:, :], count) for member in range(members)]
    first_lanes = iota((size, width), 1) < width // 2
    for k in range(count):
        here, line = slice(k * size, (k + 1) * size), slice(k, k + 1)
        values = [in_ref[member, here, :].astype(F32) for member in range(members)]
        carried = jnp.zeros((size, width), F32)
        before = []
        for member in range(members):
            before.append(carried)
            carried = over[member][line, :] * carried + values[member]
        forward = carried
        carried = jnp.zeros((size, width), F32)
        for member in reversed(range(members)):
            inner_ref[member, here, :] = jnp.where(first_lanes, before[member], carried)
            carried = over[member][line, :] * carried + values[member]
        total = jnp.where(first_lanes, forward, carried)
        total_ref[here, :] = total
        send_ref[here, :] = total
    all_over = functools.reduce(lambda a, b: a * b, over)
    decays_ref[0] = all_over
    decays_ref[1] = jnp.ones_like(all_over)
    decays_ref[2] = jnp.ones_like(all_over)
    send_ref[piece:, :] = terms_of(all_over, send_ref.shape[0] - piece)


def level_kernel(place_ref, decays_ref, total_ref, recv_ref, around_ref,
                 new_around_ref, new_decays_ref, send_ref, new_total_ref, *, size, level, top):
    group = place_ref[0] >> 3
    piece, width = total_ref.shape
    count = piece // size
    upper = (group >> level) & 1
    own, before, after = decays_ref[0], decays_ref[1], decays_ref[2]
    other = from_terms(recv_ref[piece:, :], count)
    first_lanes = iota((size, width), 1) < width // 2
    wanted = jnp.where(first_lanes, 0, 1) != upper
    for k in range(count):
        here, line = slice(k * size, (k + 1) * size), slice(k, k + 1)
        recv = recv_ref[here, :].astype(F32)
        scale = jnp.where(first_lanes, before[line, :], after[line, :])
        new = jnp.where(wanted, scale * recv, 0.0)
        new_around_ref[here, :] = new if level == 0 else around_ref[here, :] + new
        total = total_ref[here, :]
        as_lower = jnp.where(first_lanes, other[line, :] * total + recv, total + own[line, :] * recv)
        as_upper = jnp.where(first_lanes, own[line, :] * recv + total, recv + other[line, :] * total)
        total = jnp.where(upper == 0, as_lower, as_upper)
        new_total_ref[here, :] = total
        if not top:
            send_ref[here, :] = total
    new_decays_ref[0] = own * other
    new_decays_ref[1] = before * jnp.where(upper == 1, other, 1.0)
    new_decays_ref[2] = after * jnp.where(upper == 0, other, 1.0)
    if top:
        total = new_total_ref[...]
        rolled = pltpu.roll(total, width // 2, 1)
        lanes = iota((piece // 2, width), 1) < width // 2
        up = jnp.where(lanes, total[0 : piece // 2, :], rolled[piece // 2 :, :])
        down = jnp.where(lanes, rolled[0 : piece // 2, :], total[piece // 2 :, :])
        above = (group >> (level + 1)) & 1
        send_ref[...] = jnp.where(above == 0, up, down)
    else:
        send_ref[piece:, :] = terms_of(own * other, send_ref.shape[0] - piece)


def back_kernel(place_ref, decays_ref, around_ref, recv_ref, in_ref, inner_ref, out_ref, *, size, level):
    group = place_ref[0] >> 3
    piece, width = around_ref.shape
    members = in_ref.shape[0]
    count = piece // size
    upper = (group >> level) & 1
    over = [from_terms(in_ref[member, piece:, :], count) for member in range(members)]
    before, after = decays_ref[1], decays_ref[2]
    packed = recv_ref[...].astype(F32)
    rolled = pltpu.roll(packed, width // 2, 1)
    first_lanes = iota((size, width), 1) < width // 2
    wanted = jnp.where(first_lanes, 0, 1) != upper
    for k in range(count):
        here, line = slice(k * size, (k + 1) * size), slice(k, k + 1)
        start = (k % (count // 2)) * size
        there = slice(start, start + size)
        plain, turned = packed[there, :], rolled[there, :]
        if k < count // 2:
            recv = jnp.where(first_lanes, plain, turned)
        else:
            recv = jnp.where(first_lanes, turned, plain)
        scale = jnp.where(first_lanes, before[line, :], after[line, :])
        arrived = around_ref[here, :] + jnp.where(wanted, scale * recv, 0.0)
        ahead = [jnp.ones((1, width), F32)]
        for member in range(members - 1):
            ahead.append(ahead[-1] * over[member][line, :])
        behind = jnp.ones((1, width), F32)
        for member in reversed(range(members)):
            scale = jnp.where(first_lanes, ahead[member], behind)
            out_ref[member, here, :] = inner_ref[member, here, :] + scale * arrived
            behind = behind * over[member][line, :]


def fetch_columns(sources, targets, sems):
    copies = []
    for source, target, sem in zip(sources, targets, sems):
        groups = sem.shape[0]
        wide = target.shape[1] // groups
        copies.append([
            pltpu.make_async_copy(
                source.at[:, pl.ds(k * wide, wide)], target.at[:, pl.ds(k * wide, wide)], sem.at[k]
            )
            for k in range(groups)
        ])
    for group in zip(*copies):
        for copy in group:
            copy.start()
    return list(zip(*copies))


def scale_kernel(x_hbm, grad_hbm, dt_t_ref, running_t_ref, scaled_ref, x_ref, grad_ref,
                 x_sems, grad_sems):
    arriving = fetch_columns((x_hbm, grad_hbm), (x_ref, grad_ref), (x_sems, grad_sems))
    heads, tokens = running_t_ref.shape
    wide = x_ref.shape[1] // len(arriving)
    size = x_ref.shape[1] // heads
    running_t = running_t_ref[...]
    to_end = (dt_t_ref[...] * jnp.exp(running_t[:, tokens - 1 : tokens] - running_t)).T
    from_start = jnp.exp(running_t).T
    lanes_first = iota((tokens, 2 * size), 1) < size
    for pair in range(heads // 2):
        lanes = slice(2 * size * pair, 2 * size * (pair + 1))
        if lanes.start % wide == 0:
            for copy in arriving[lanes.start // wide]:
                copy.wait()
        even, odd = slice(2 * pair, 2 * pair + 1), slice(2 * pair + 1, 2 * pair + 2)
        x_scale = jnp.where(lanes_first, to_end[:, even], to_end[:, odd])
        grad_scale = jnp.where(lanes_first, from_start[:, even], from_start[:, odd])
        x_high, x_low = split(x_ref[:, lanes].astype(F32) * x_scale)
        grad_high, grad_low = split(grad_ref[:, lanes].astype(F32) * grad_scale)
        for k, value in enumerate((x_high, grad_high, x_low, grad_low)):
            scaled_ref[k * tokens : (k + 1) * tokens, lanes] = value


def pairs_kernel(projected_ref, x_hbm, grad_hbm, dt_t_ref, running_t_ref, d_proj_ref,
                 x_ref, grad_ref, pair_ref, x_sems, grad_sems):
    arriving = fetch_columns((x_hbm, grad_hbm), (x_ref, grad_ref), (x_sems, grad_sems))
    heads, tokens = running_t_ref.shape
    rows = tokens // 2
    wide = x_ref.shape[1] // len(arriving)
    size = x_ref.shape[1] // heads
    width = projected_ref.shape[1]
    running_t = running_t_ref[...]
    running = running_t.T
    dt_t = dt_t_ref[...]
    causal = iota((rows, rows), 0) >= iota((rows, rows), 1)
    lanes_first = iota((tokens, 2 * size), 1) < size
    pair_ref[...] = jnp.zeros_like(pair_ref)
    for pair in range(heads // 2):
        lanes = slice(2 * size * pair, 2 * size * (pair + 1))
        if lanes.start % wide == 0:
            for copy in arriving[lanes.start // wide]:
                copy.wait()
        x = x_ref[:, lanes]
        grad = grad_ref[:, lanes]
        zero = jnp.zeros_like(grad)
        both = jnp.concatenate(
            [jnp.where(lanes_first, grad, zero), jnp.where(lanes_first, zero, grad)], axis=0
        )
        products = mm_nt(both, x)
        for at, to in ((0, 0), (1, 0), (1, 1)):
            here, there = slice(at * rows, (at + 1) * rows), slice(to * rows, (to + 1) * rows)
            total = pair_ref[here, there]
            for side, head in enumerate((2 * pair, 2 * pair + 1)):
                spread = running[here, head : head + 1] - running_t[head : head + 1, there]
                if at == to:
                    spread = jnp.where(causal, spread, NEG)
                start = side * tokens + at * rows
                part = products[start : start + rows, there]
                total = total + jnp.exp(spread) * (part * dt_t[head : head + 1, there])
            pair_ref[here, there] = total
    high, low = split(projected_ref[...])
    both = jnp.concatenate([high, low], axis=1)

    def product(weights):
        weights_high, weights_low = split(weights)
        by_both = mm(weights_high, both)
        return by_both[:, :width] + by_both[:, width:] + mm(weights_low, high)

    pair_sum = pair_ref[...]
    onto_c, onto_b = product(pair_sum), product(pair_sum.T)
    first = iota((tokens, width), 1) < width // 2
    d_proj_ref[...] = pltpu.roll(jnp.where(first, onto_c, onto_b), width // 2, 1)


def inside_kernel(projected_ref, grad_hbm, running_t_ref, d_in_ref, grad_ref, grad_sems):
    arriving = fetch_columns((grad_hbm,), (grad_ref,), (grad_sems,))
    heads, tokens = running_t_ref.shape
    wide = grad_ref.shape[1] // len(arriving)
    size = grad_ref.shape[1] // heads
    rows = tokens // 2
    width = projected_ref.shape[1]
    projected = projected_ref[...]
    swapped = pltpu.roll(projected, width // 2, 1)
    first = iota(projected.shape, 1) < width // 2
    scores_t = mm_nt(jnp.where(first, projected, 0.0), swapped, HIGH)
    running_t = running_t_ref[...]
    running = running_t.T
    later = iota((rows, rows), 1) >= iota((rows, rows), 0)
    lanes_first = iota((rows, 2 * size), 1) < size
    for pair in range(heads // 2):
        lanes = slice(2 * size * pair, 2 * size * (pair + 1))
        if lanes.start % wide == 0:
            for copy in arriving[lanes.start // wide]:
                copy.wait()
        apart = []
        for part in range(2):
            grad = grad_ref[part * rows : (part + 1) * rows, lanes]
            zero = jnp.zeros_like(grad)
            apart.append((jnp.where(lanes_first, grad, zero), jnp.where(lanes_first, zero, grad)))
        for at in range(2):
            here = slice(at * rows, (at + 1) * rows)
            weights, sources = [], []
            for to in range(at, 2):
                there = slice(to * rows, (to + 1) * rows)
                for side, head in enumerate((2 * pair, 2 * pair + 1)):
                    spread = running_t[head : head + 1, there] - running[here, head : head + 1]
                    if at == to:
                        spread = jnp.where(later, spread, NEG)
                    weights.append((jnp.exp(spread) * scores_t[here, there]).astype(BF16))
                    sources.append(apart[to][side])
            d_in_ref[here, lanes] = mm(
                jnp.concatenate(weights, axis=1), jnp.concatenate(sources, axis=0)
            )


def cross_kernel(arrived_ref, scaled_ref, d_proj_ref, out_ref):
    tokens, width = d_proj_ref.shape
    onto = mm(scaled_ref[...], jnp.concatenate(split(arrived_ref[...]), axis=1))
    onto = onto[:, :width] + onto[:, width:]
    onto = onto[0 : 2 * tokens, :] + onto[2 * tokens :, :]
    first = iota((tokens, width), 1) < width // 2
    crossing = jnp.where(first, onto[tokens:, :], onto[:tokens, :])
    out_ref[...] = d_proj_ref[...] + pltpu.roll(crossing, width // 2, 1)


def term_kernel(mine_ref, other_ref, hidden_t_ref, d_low_ref, term_hbm, term_ref, sems):
    chips, chunk, _ = term_ref.shape
    rows = hidden_t_ref.shape[0] // chips
    d_low = (mine_ref[...] + other_ref[...]).astype(BF16)
    d_low_ref[...] = d_low
    parts = sems.shape[0]
    stores = []
    for part in range(parts):
        first, count = part * chips // parts, chips // parts
        term = mm(hidden_t_ref[first * rows : (first + count) * rows, :], d_low)
        for k in range(count):
            block = term[k * rows : (k + 1) * rows, :]
            high = block.astype(BF16).astype(F32)
            rest = (block - high)[0 : chunk - rows, :]
            term_ref[first + k] = jnp.concatenate([high, rest], axis=0).astype(BF16)
        there = pl.ds(first, count)
        stores.append(pltpu.make_async_copy(term_ref.at[there], term_hbm.at[there], sems.at[part]))
        stores[-1].start()
    for store in stores:
        store.wait()


def inputs_kernel(place_ref, arrived_ref, projected_ref, d_in_ref, dt_t_ref, running_t_ref, *rest, other):
    if other:
        (grad_ref,) = rest
    else:
        d_low_ref, w_hbm, grad_ref, grad_hidden_ref, w_ref, sem = rest
        fetch = pltpu.make_async_copy(w_hbm, w_ref, sem.at[0])
        fetch.start()
    heads, tokens = dt_t_ref.shape
    rows = tokens // 2
    width = projected_ref.shape[1]
    size = arrived_ref.shape[0] // heads
    core = place_ref[0] & 1
    which = 1 - core if other else core
    here = pl.ds(pl.multiple_of(which * rows, rows), rows)
    swapped = pltpu.roll(projected_ref[here, :], width // 2, 1)
    first = iota((rows, width), 1) < width // 2
    b_high, b_low = split(jnp.where(first, 0.0, swapped))
    b_both = jnp.concatenate([b_high, b_low], axis=0)
    running_t = running_t_ref[...]
    to_end_t = jnp.exp(running_t[:, tokens - 1 : tokens] - running_t)

    def columns(both):
        return jnp.where(which == 0, both[:, :rows], both[:, rows:]).T

    dt, to_end = columns(dt_t_ref[...]), columns(to_end_t)
    lanes_first = iota((rows, 2 * size), 1) < size
    for pair in range(heads // 2):
        lanes = slice(2 * size * pair, 2 * size * (pair + 1))
        even, odd = 2 * pair, 2 * pair + 1
        crossing = mm_nt(b_both, arrived_ref[lanes, :].astype(BF16))
        crossing = crossing[:rows, :] + crossing[rows:, :]
        decay = jnp.where(lanes_first, to_end[:, even : even + 1], to_end[:, odd : odd + 1])
        step = jnp.where(lanes_first, dt[:, even : even + 1], dt[:, odd : odd + 1])
        grad_ref[:, lanes] = step * (d_in_ref[here, lanes] + decay * crossing)
    if not other:
        fetch.wait()
        grad_hidden_ref[...] = mm_nt(
            d_low_ref[here, :], w_ref[...].reshape(grad_hidden_ref.shape[1], width)
        )


def join_kernel(place_ref, mine_ref, other_ref, out_hbm, sems):
    core = place_ref[0] & 1
    half = mine_ref.shape[1]
    copies = []
    for k, (source, there) in enumerate(((mine_ref, core), (other_ref, 1 - core))):
        lanes = pl.ds(pl.multiple_of(there * half, half), half)
        copies.append(pltpu.make_async_copy(source, out_hbm.at[:, lanes], sems.at[k]))
    for copy in copies:
        copy.start()
    for copy in copies:
        copy.wait()


def sum_kernel(terms_ref, out_ref, *, scale):
    rows = out_ref.shape[0]
    more = terms_ref.shape[1] - rows
    terms = jnp.sum(terms_ref[...].astype(F32), axis=0)
    out_ref[0:more, :] = (terms[0:more, :] + terms[rows:, :]) * scale
    out_ref[more:, :] = terms[more:rows, :] * scale


def per_device(hidden, x_act, dt_step, log_decay, w_bc, grad_y):
    devices = lax.axis_size("outer") * lax.axis_size("inner")
    rows, model = hidden.shape
    heads = dt_step.shape[1]
    flat = x_act.shape[1]
    w_rows, width = w_bc.shape
    half = flat // 2
    own_heads = heads // 2
    tokens = 2 * rows
    chips = devices // 2
    size = flat // heads
    levels = (chips // 4).bit_length() - 1
    piece = half // 4
    count = piece // size
    decay_rows = -(-3 * count // 16) * 16
    position = lax.axis_index("outer") * lax.axis_size("inner") + lax.axis_index("inner")
    place = position.astype(jnp.int32).reshape(1)
    same_core = [list(range(core, devices, 2)) for core in range(2)]
    same_group = [
        list(range(first + core, first + 8, 2)) for first in range(0, devices, 8) for core in range(2)
    ]

    def exchange(array, among):
        return lax.all_to_all(
            array, AXES, split_axis=0, concat_axis=0, tiled=True, axis_index_groups=among
        )

    def swap(array, apart=1):
        return lax.ppermute(array, AXES, [(i, i ^ apart) for i in range(devices)])

    spread, small = call(
        spread_kernel,
        (pltpu.HBM((devices, w_rows, width), BF16), shaped((2, heads, rows), F32)), [HBM] * 3,
        [pltpu.VMEM((w_rows, width), BF16), pltpu.VMEM((devices, w_rows, width), BF16),
         pltpu.SemaphoreType.DMA((4,))],
        (HBM, VMEM),
    )(in_hbm(w_bc), in_hbm(dt_step.T), in_hbm(log_decay.T))
    weights = lax.all_to_all(spread, AXES, split_axis=0, concat_axis=0, tiled=True)
    in_kernel = w_rows % 16 == 0
    groups = 4
    hidden_other = swap(hidden)
    hidden_t_rows = model // 2 if in_kernel else 16
    (scaled_t, running_t, dt_t, hidden_both, hidden_t, x_both, grad_both) = call(
        functools.partial(prelude_kernel, parts=w_rows if in_kernel else 0),
        (shaped((half, 4 * tokens), BF16), shaped((own_heads, tokens), F32), pltpu.HBM((own_heads, tokens), F32),
         shaped((tokens, model), BF16), pltpu.HBM((hidden_t_rows, tokens), BF16),
         pltpu.HBM((tokens, half), BF16), pltpu.HBM((tokens, half), BF16)),
        [SMEM] + [HBM] * 4 + [VMEM] * 2 + [HBM] * 2,
        [pltpu.VMEM((tokens, half), BF16), pltpu.VMEM((tokens, half), BF16),
         pltpu.VMEM((model, tokens), BF16), pltpu.VMEM((hidden_t_rows, tokens), BF16),
         pltpu.VMEM((own_heads, tokens), F32),
         pltpu.SemaphoreType.DMA((2, groups)), pltpu.SemaphoreType.DMA((2, groups)),
         pltpu.SemaphoreType.DMA((2,)), pltpu.SemaphoreType.DMA((4,))],
        (VMEM, VMEM, HBM, VMEM, HBM, HBM, HBM),
    )(place, in_hbm(x_act), in_hbm(swap(x_act)), in_hbm(grad_y), in_hbm(swap(grad_y)),
      small, swap(small), in_hbm(hidden), hidden_other)
    if not in_kernel:
        weights = weights.reshape(model, width)
        both = jnp.where(place[0] % 2 == 0, jnp.concatenate([hidden, hidden_other], axis=0),
                         jnp.concatenate([hidden_other, hidden], axis=0))
        hidden_t = both.T.reshape(chips, 2, w_rows, tokens)
        hidden_t = jnp.where(place[0] % 2 == 0, hidden_t[:, 0], hidden_t[:, 1])
        hidden_t = hidden_t.reshape(model // 2, tokens)
    projected, slices = call(
        states_kernel,
        (shaped((tokens, width), F32), shaped((4, piece + decay_rows, width), F32)),
        [VMEM] * 4,
    )(hidden_both, weights, scaled_t, running_t)
    slices = exchange(slices, same_group)
    part, decay_part = shaped((piece, width), F32), shaped((3, count, width), F32)
    climb = shaped((piece + decay_rows, width), F32)
    total, inner, decays, send = call(
        functools.partial(group_kernel, size=size),
        (part, shaped((4, piece, width), F32), decay_part, climb), [VMEM],
    )(slices)
    around = total
    for level in range(levels - 1):
        come = swap(send, 8 << level)
        top = level == levels - 2
        kernel = functools.partial(level_kernel, size=size, level=level, top=top)
        if top:
            around, decays, send = call(
                kernel, (part, decay_part, shaped((piece // 2, width), F32)),
                [SMEM] + [VMEM] * 4, [pltpu.VMEM((piece, width), F32)],
            )(place, decays, total, come, around)
        else:
            around, decays, send, total = call(
                kernel, (part, decay_part, climb, part), [SMEM] + [VMEM] * 4
            )(place, decays, total, come, around)
    come = swap(send, 4 << levels)
    homeward = call(
        functools.partial(back_kernel, size=size, level=levels - 1),
        shaped((4, piece, width), F32), [SMEM] + [VMEM] * 5,
    )(place, decays, around, come, slices, inner)
    x_both, grad_both = in_hbm(x_both), in_hbm(grad_both)
    buffer = pltpu.VMEM((tokens, half), BF16)
    sems = pltpu.SemaphoreType.DMA((groups,))
    scaled = call(
        scale_kernel, shaped((4 * tokens, half), BF16), [HBM] * 2 + [VMEM] * 2,
        [buffer, buffer, sems, sems],
    )(x_both, grad_both, dt_t, running_t)
    d_inside = call(
        pairs_kernel, shaped((tokens, width), F32), [VMEM] + [HBM] * 2 + [VMEM] * 2,
        [buffer, buffer, pltpu.VMEM((tokens, tokens), F32), sems, sems],
    )(projected, x_both, grad_both, dt_t, running_t)
    d_in = call(
        inside_kernel, shaped((tokens, half), F32), [VMEM, HBM, VMEM], [buffer, sems]
    )(projected, grad_both, running_t)
    arrived = exchange(homeward, same_group).reshape(half, width)
    d_part = call(cross_kernel, shaped((tokens, width), F32), [VMEM] * 3)(arrived, scaled, d_inside)
    term_rows = w_rows + w_rows // 2
    d_low, term = call(
        term_kernel,
        (shaped((tokens, width), BF16), pltpu.HBM((chips, term_rows, width), BF16)), [VMEM] * 3,
        [pltpu.VMEM((chips, term_rows, width), BF16), pltpu.SemaphoreType.DMA((4,))], (VMEM, HBM),
    )(d_part, swap(d_part), hidden_t)
    terms = exchange(term, same_core)
    in_specs = [SMEM] + [VMEM] * 5
    send = call(
        functools.partial(inputs_kernel, other=True), shaped((rows, half), F32), in_specs
    )(place, arrived, projected, d_in, dt_t, running_t)
    come = swap(send)
    mine, grad_hidden = call(
        functools.partial(inputs_kernel, other=False),
        (shaped((rows, half), F32), shaped((rows, model), F32)), in_specs + [VMEM, HBM],
        [pltpu.VMEM(weights.shape, BF16), pltpu.SemaphoreType.DMA((1,))],
    )(place, arrived, projected, d_in, dt_t, running_t, d_low, in_hbm(weights))
    grad_x = call(
        join_kernel, pltpu.HBM((rows, flat), F32), [SMEM] + [VMEM] * 2,
        [pltpu.SemaphoreType.DMA((2,))], HBM,
    )(place, mine, come)
    scale = 1.0 / math.sqrt(rows * devices)
    grad_proj = call(
        functools.partial(sum_kernel, scale=scale), shaped((w_rows, width), F32), [VMEM]
    )(terms)
    return (grad_x, grad_hidden, grad_proj)


def solution(mesh):
    spec = P(AXES, None)

    return jax.shard_map(
        per_device, mesh=mesh, in_specs=(spec,) * 6, out_specs=(spec,) * 3, check_vma=False
    )
```
